32 devices in a mesh: groups: 2 (over x), tensor: 4 (over y, core), dp: 4 (over z).
Axes of the slice: x: 2, y: 2, z: 4, core: 2. Of those that a mesh axis runs over, the one named last changes fastest.
Arguments:
- first_out: bfloat16 [4096, 1024], P(('groups', 'tensor', 'dp')), parts along dimension 0, may hold values from -6 to 6
- second_out: bfloat16 [4096, 1024], P(('groups', 'tensor', 'dp')), parts along dimension 0, may hold values from -6 to 6
- grad_first: bfloat16 [4096, 1024], P(('groups', 'tensor', 'dp')), parts along dimension 0, may hold values from -6 to 6
- grad_second: bfloat16 [4096, 1024], P(('groups', 'tensor', 'dp')), parts along dimension 0, may hold values from -6 to 6
- w_up: bfloat16 [1024, 8192], P('dp', 'tensor'), may hold values from -0.1875 to 0.1875
- w_down: bfloat16 [8192, 1024], P('tensor', 'dp'), may hold values from -0.0625 to 0.0625
- norm_gain: float32 [1024], replicated, may hold values from 0.25 to 1.75
- norm_bias: float32 [1024], replicated, may hold values from -3 to 3
Outputs:
- second_in: bfloat16 [4096, 1024], P(('groups', 'tensor', 'dp')), parts along dimension 0
- grad_first_in: float32 [4096, 1024], P(('groups', 'tensor', 'dp')), parts along dimension 0
- grad_up: float32 [2048, 8192], P(('groups', 'dp'), 'tensor'), parts along dimension 0
- grad_down: float32 [16384, 1024], P(('groups', 'tensor'), 'dp'), parts along dimension 0
- grad_norm: float32 [4, 1024], P('groups'), parts along dimension 0
The draws below stay inside these ranges and needn't reach their ends.
There are 2 independent parts, one for each index of `groups`. The reference program is written for one: setup_inputs(seed, part) draws one part's arguments, and reference() takes and returns one part's arrays. A program takes and returns all parts, laid end to end along the dimension named above; an argument that names none is the same for every part. Nothing has to cross between parts.
All inputs are finite; a program needn't handle non-finite values.
Results may differ from the reference program's by a relative error of at most 0.017.
Values may be sent and summed in bfloat16 or wider, within the bound.
A program may use at most 64 MiB of HBM per device.

```python
import jax
import jax.numpy as jnp
from jax import lax

D = 1024
FF = 8192
TOKENS = 2048
N_TENSOR = 4


def block_scale(key, dims, split, least, top_value):
    level, own = 1.0, jax.random.fold_in(key, 6)
    for dim, shards_of in split:
        heights = jnp.exp(jax.random.uniform(jax.random.fold_in(own, dim), (shards_of,), jnp.float32, least / len(split), top_value / len(split)))
        level = level * jnp.repeat(heights, dims[dim] // shards_of).reshape([-1 if axis == dim else 1 for axis in range(len(dims))])
    return level


def noise(rng, extent, width, limit, shards=(), kind=jnp.bfloat16):
    loudness = block_scale(rng, extent, shards, -0.22, 0.18) if shards else 1.0
    result = jax.random.normal(rng, extent, jnp.float32) * width * loudness
    return jnp.minimum(jnp.maximum(result, -limit), limit).astype(kind)


def setup_inputs(seed: int = 0, part: int = 0) -> dict:
    splits = jax.random.split(jax.random.key(seed), 9)
    part_splits = jax.random.split(jax.random.fold_in(splits[8], part), 9)
    first_out = noise(part_splits[0], (TOKENS, D), 1.0, 6.0, ((0, 16),))
    second_out = noise(part_splits[1], (TOKENS, D), 1.0, 6.0, ((0, 16),))
    grad_first = noise(part_splits[2], (TOKENS, D), 1.0, 6.0, ((0, 16),))
    grad_second = noise(part_splits[3], (TOKENS, D), 1.0, 6.0, ((0, 16),))
    w_up = noise(splits[4], (D, FF), D ** -0.5, 0.1875, ((0, 4), (1, 4)))
    w_down = noise(splits[5], (FF, D), FF ** -0.5, 0.0625, ((0, 4), (1, 4)))
    norm_gain = jnp.clip(1.0 + 0.15 * jax.random.normal(splits[6], (D,), jnp.float32), 0.25, 1.75)
    norm_bias = noise(splits[7], (D,), 0.5, 3.0, (), jnp.float32)
    return dict(first_out=first_out, second_out=second_out, grad_first=grad_first, grad_second=grad_second, w_up=w_up, w_down=w_down, norm_gain=norm_gain, norm_bias=norm_bias)


epsilon = 1e-06

def normalize(row_data, norm_gain, norm_bias):
    values = row_data.astype(jnp.float32)
    row_mean = lax.optimization_barrier(jnp.mean(values, axis=-1, keepdims=True))
    centred = values - row_mean
    inv_std = lax.rsqrt(lax.optimization_barrier(jnp.mean(centred * centred, axis=-1, keepdims=True)) + epsilon)
    standard = centred * inv_std
    normed = (standard * norm_gain.astype(jnp.float32) + norm_bias.astype(jnp.float32)).astype(jnp.bfloat16)
    return (standard, inv_std, normed)

def round_half(values):
    return lax.optimization_barrier(values.astype(jnp.bfloat16)).astype(jnp.float32)

def reference(first_out, second_out, grad_first, grad_second, w_up, w_down, norm_gain, norm_bias):
    standard, inv_std, normed = normalize(first_out, norm_gain, norm_bias)
    block_width = FF // N_TENSOR
    up_blocks = jnp.transpose(w_up.reshape(D, N_TENSOR, block_width), (1, 0, 2))
    down_blocks = w_down.reshape(N_TENSOR, block_width, D)

    def step_block(totals, blocks):
        branch, grad_normed = totals
        up_block, down_block = blocks
        preact = jnp.dot(normed, up_block, preferred_element_type=jnp.float32)
        hidden = jax.nn.gelu(preact).astype(jnp.bfloat16)
        branch = branch + round_half(jnp.dot(hidden, down_block, preferred_element_type=jnp.float32))
        grad_hidden = lax.dot_general(grad_second, down_block, (((1,), (1,)), ((), ())), preferred_element_type=jnp.float32)
        grad_pre = jax.vjp(jax.nn.gelu, preact)[1](grad_hidden)[0].astype(jnp.bfloat16)
        grad_down = lax.dot_general(hidden, grad_second, (((0,), (0,)), ((), ())), preferred_element_type=jnp.float32)
        grad_up = lax.dot_general(normed, grad_pre, (((0,), (0,)), ((), ())), preferred_element_type=jnp.float32)
        grad_normed = grad_normed + round_half(lax.dot_general(grad_pre, up_block, (((1,), (1,)), ((), ())), preferred_element_type=jnp.float32))
        return ((branch, grad_normed), (grad_up, grad_down))
    empty_rows = jnp.zeros((TOKENS, D), jnp.float32)
    (branch, grad_normed), (up_grads, down_grads) = lax.scan(step_block, (empty_rows, empty_rows), (up_blocks, down_blocks))
    grad_scale = TOKENS ** (-0.5)
    second_in = (second_out.astype(jnp.float32) - branch).astype(jnp.bfloat16)
    grad_std = grad_normed * norm_gain.astype(jnp.float32)
    grad_rows = inv_std * (grad_std - lax.optimization_barrier(jnp.mean(grad_std, axis=-1, keepdims=True)) - standard * lax.optimization_barrier(jnp.mean(grad_std * standard, axis=-1, keepdims=True)))
    grad_first_in = grad_first.astype(jnp.float32) + grad_rows
    grad_norm = jnp.stack([lax.optimization_barrier(jnp.sum(grad_normed * standard, axis=0)), lax.optimization_barrier(jnp.sum(grad_normed, axis=0))]) * grad_scale
    grad_up = jnp.transpose(up_grads, (1, 0, 2)).reshape(D, FF) * grad_scale
    grad_down = down_grads.reshape(FF, D) * grad_scale
    return (second_in, grad_first_in, grad_up, grad_down, grad_norm)
```

```python
import functools

import jax
import jax.numpy as jnp
from jax import lax
from jax.experimental import pallas as pl
from jax.experimental.pallas import tpu as pltpu
from jax.sharding import PartitionSpec as P

epsilon = 1e-06


def normalize(row_data, norm_gain, norm_bias):
    values = row_data.astype(jnp.float32)
    row_mean = jnp.mean(values, axis=-1, keepdims=True)
    centred = values - row_mean
    inv_std = lax.rsqrt(jnp.mean(centred * centred, axis=-1, keepdims=True) + epsilon)
    standard = centred * inv_std
    normed = (standard * norm_gain + norm_bias).astype(jnp.bfloat16)
    return (standard, inv_std, normed)


def contract_tokens(left_rows, right_rows):
    return lax.dot_general(
        left_rows, right_rows, (((0,), (0,)), ((), ())), preferred_element_type=jnp.float32
    )


def body(first_out, second_out, grad_first, grad_second, w_up, w_down, norm_gain, norm_bias):
    own_rows = first_out.shape[0]
    up_full, down_full = (
        lax.all_gather(w_up, "dp", axis=0, tiled=True),
        lax.all_gather(w_down, "dp", axis=1, tiled=True),
    )
    first_all, grad_all = (
        lax.all_gather(first_out, "tensor", axis=0, tiled=True),
        lax.all_gather(grad_second, "tensor", axis=0, tiled=True),
    )
    standard_all, inv_std_all, normed = normalize(first_all, norm_gain, norm_bias)
    offset = lax.axis_index("tensor") * own_rows
    standard = lax.dynamic_slice_in_dim(standard_all, offset, own_rows, 0)
    inv_std = lax.dynamic_slice_in_dim(inv_std_all, offset, own_rows, 0)
    preact = jnp.dot(normed, up_full, preferred_element_type=jnp.float32)
    hidden = jax.nn.gelu(preact).astype(jnp.bfloat16)
    branch = lax.psum_scatter(
        jnp.dot(hidden, down_full, preferred_element_type=jnp.float32).astype(jnp.bfloat16),
        "tensor",
        scatter_dimension=0,
        tiled=True,
    ).astype(jnp.float32)
    second_in = (second_out.astype(jnp.float32) - branch).astype(jnp.bfloat16)
    tokens = own_rows * lax.axis_size("tensor") * lax.axis_size("dp")
    grad_scale = tokens ** (-0.5)
    grad_down_part = contract_tokens(hidden, grad_all)
    grad_down = (
        lax.psum_scatter(
            grad_down_part.astype(jnp.bfloat16), "dp", scatter_dimension=1, tiled=True
        ).astype(jnp.float32)
        * grad_scale
    )
    grad_hidden = lax.dot_general(
        grad_all, down_full, (((1,), (1,)), ((), ())), preferred_element_type=jnp.float32
    )
    grad_pre = jax.vjp(jax.nn.gelu, preact)[1](grad_hidden)[0].astype(jnp.bfloat16)
    grad_up_part = contract_tokens(normed, grad_pre)
    grad_up = (
        lax.psum_scatter(
            grad_up_part.astype(jnp.bfloat16), "dp", scatter_dimension=0, tiled=True
        ).astype(jnp.float32)
        * grad_scale
    )
    grad_normed = lax.psum_scatter(
        lax.dot_general(
            grad_pre, up_full, (((1,), (1,)), ((), ())), preferred_element_type=jnp.float32
        ).astype(jnp.bfloat16),
        "tensor",
        scatter_dimension=0,
        tiled=True,
    ).astype(jnp.float32)
    grad_std = grad_normed * norm_gain
    grad_rows = inv_std * (
        grad_std
        - jnp.mean(grad_std, axis=-1, keepdims=True)
        - standard * jnp.mean(grad_std * standard, axis=-1, keepdims=True)
    )
    grad_first_in = grad_first.astype(jnp.float32) + grad_rows
    local_stats = jnp.stack([jnp.sum(grad_normed * standard, axis=0), jnp.sum(grad_normed, axis=0)])
    grad_norm = lax.psum(local_stats, ("tensor", "dp")) * grad_scale
    return (second_in, grad_first_in, grad_up, grad_down, grad_norm)


def span(index, size):
    return pl.ds(pl.multiple_of(index * size, size), size)


def flipped(index, mask, bits):
    for bit in range(bits):
        if mask >> bit & 1:
            step = 1 << bit
            index = index + (1 - 2 * ((index // step) % 2)) * step
    return index


def greet(n_groups, n_dp, bits, group, tensor, dp):
    barrier = pltpu.get_barrier_semaphore()
    peers = [{"dp": (dp + s) % n_dp} for s in range(1, n_dp)]
    peers += [{"tensor": flipped(tensor, 1 << bit, bits)} for bit in range(bits)]
    peers += [{"groups": (group + s) % n_groups} for s in range(1, n_groups)]
    for peer in peers:
        pl.semaphore_signal(
            barrier, inc=1, device_id=peer, device_id_type=pl.DeviceIdType.MESH
        )
    pl.semaphore_wait(barrier, len(peers))


def remote(src, dst, sems, index, peer):
    return pltpu.make_async_remote_copy(
        src_ref=src,
        dst_ref=dst,
        send_sem=sems[0].at[index],
        recv_sem=sems[1].at[index],
        device_id=peer,
        device_id_type=pl.DeviceIdType.MESH,
    )


def gather_kernel(
    n_groups, n_tensor, n_dp,
    normed_ref, grad_ref, w_up_ref, w_down_ref,
    normed_all, grad_all, up_ref, down_ref,
    local_sem, line_send, line_recv, column_send, column_recv,
    weight_send, weight_recv, share_send, share_recv,
):
    group, tensor, dp = (lax.axis_index(name) for name in ("groups", "tensor", "dp"))
    bits = n_tensor.bit_length() - 1
    rows = normed_ref.shape[0]
    depth = w_up_ref.shape[0]
    units = w_up_ref.shape[1] // n_dp
    inputs, outputs = (normed_ref, grad_ref), (normed_all, grad_all)
    line_sems, column_sems = (line_send, line_recv), (column_send, column_recv)
    weight_sems, share_sems = (weight_send, weight_recv), (share_send, share_recv)

    def block(a, mask, source):
        return outputs[a].at[span(flipped(tensor, mask, bits) * n_dp + source, rows), :]

    def place(k):
        if k == 0:
            return dp, None
        if k < n_dp:
            return dp - k, dp >= k
        return dp + (k - n_dp + 1), dp + (k - n_dp + 1) <= n_dp - 1

    def guarded(conditions, action):
        conditions = [c for c in conditions if c is not None]
        if not conditions:
            action()
        else:
            pl.when(functools.reduce(jnp.logical_and, conditions))(action)

    def line_copy(a, side, distance):
        if side == 0:
            source, target = dp - (distance - 1), dp + 1
        else:
            source, target = dp + (distance - 1), dp - 1
        src = inputs[a] if distance == 1 else block(a, 0, source)
        return remote(src, block(a, 0, source), line_sems, (a, side, distance), {"dp": target})

    def line_send_conditions(side, distance):
        if side == 0:
            return [dp >= distance - 1 if distance > 1 else None, dp <= n_dp - 2]
        return [dp <= n_dp - distance if distance > 1 else None, dp >= 1]

    def column_copy(a, mask, k, bit):
        source, _ = place(k)
        src = inputs[a] if mask == 0 and k == 0 else block(a, mask, source)
        return remote(
            src, block(a, mask, source), column_sems, (a, mask | 1 << bit, k),
            {"tensor": flipped(tensor, 1 << bit, bits)},
        )

    def column_arrival(a, mask, k):
        source, _ = place(k)
        bit = (mask & -mask).bit_length() - 1
        here = block(a, mask, source)
        return remote(
            here, here, column_sems, (a, mask, k), {"tensor": flipped(tensor, 1 << bit, bits)}
        )

    def next_bits(mask):
        top = bits if mask == 0 else (mask & -mask).bit_length() - 1
        return list(reversed(range(top)))

    def pass_on(a, mask, k):
        for bit in next_bits(mask):
            column_copy(a, mask, k, bit).start()

    part = depth // n_groups
    piece = units // n_groups

    def weight_views(kind, source, owner):
        if kind == 0:
            return up_ref.at[span(source * n_groups + owner, part), :]
        return down_ref.at[span(owner, piece), span(source, depth)]

    def weight_copy(kind, s):
        target = (dp + s) % n_dp
        if kind == 0:
            src = w_up_ref.at[span(group, part), span(target, units)]
        else:
            src = w_down_ref.at[span(target * n_groups + group, piece), :]
        return remote(src, weight_views(kind, dp, group), weight_sems, (kind, s), {"dp": target})

    def weight_arrival(kind, s):
        here = weight_views(kind, (dp + n_dp - s) % n_dp, group)
        return remote(here, here, weight_sems, (kind, s), {"dp": (dp + s) % n_dp})

    def share_copy(kind, s, h):
        here = weight_views(kind, (dp + n_dp - s) % n_dp, group)
        return remote(here, here, share_sems, (kind, s, h), {"groups": (group + h) % n_groups})

    def share_arrival(kind, s, h):
        here = weight_views(kind, (dp + n_dp - s) % n_dp, (group + n_groups - h) % n_groups)
        return remote(here, here, share_sems, (kind, s, h), {"groups": (group + h) % n_groups})

    greet(n_groups, n_dp, bits, group, tensor, dp)
    order = [0] + [k for s in range(1, n_dp) for k in (s, s + n_dp - 1)]
    for a in range(2):
        for side in range(2):
            guarded(line_send_conditions(side, 1), lambda a=a, side=side: line_copy(a, side, 1).start())
        pass_on(a, 0, 0)
    for s in range(1, n_dp):
        for kind in range(2):
            weight_copy(kind, s).start()
    local = [
        pltpu.make_async_copy(inputs[a], block(a, 0, dp), local_sem.at[a]) for a in range(2)
    ]
    local.append(
        pltpu.make_async_copy(
            w_up_ref.at[:, span(dp, units)], up_ref.at[span(dp, depth), :], local_sem.at[2]
        )
    )
    local.append(
        pltpu.make_async_copy(
            w_down_ref.at[span(dp, units), :], down_ref.at[:, span(dp, depth)], local_sem.at[3]
        )
    )
    for copy in local:
        copy.start()

    through = [m for m in range(1, n_tensor) if next_bits(m)]
    final = [m for m in range(1, n_tensor) if not next_bits(m)]

    def relay(k):
        for a in range(2):
            for mask in sorted(through, reverse=True):
                def action(a=a, mask=mask):
                    column_arrival(a, mask, k).wait_recv()
                    pass_on(a, mask, k)
                guarded([place(k)[1]], action)

    done = [[0]] + [[s, s + n_dp - 1] for s in range(1, n_dp)]
    for s in range(1, n_dp):
        for a in range(2):
            for side in range(2):
                k = done[s][side]

                def action(a=a, side=side, k=k, s=s):
                    source, _ = place(k)
                    here = block(a, 0, source)
                    remote(here, here, line_sems, (a, side, s), {"dp": (dp + 1) % n_dp}).wait_recv()
                    if s < n_dp - 1:
                        guarded(
                            line_send_conditions(side, s + 1),
                            lambda: line_copy(a, side, s + 1).start(),
                        )
                    pass_on(a, 0, k)

                guarded([place(k)[1]], action)
        for k in done[s - 1]:
            relay(k)
        for kind in range(2):
            weight_arrival(kind, s).wait_recv()
            for h in range(1, n_groups):
                share_copy(kind, s, h).start()
    for k in done[n_dp - 1]:
        relay(k)
    for k in order:
        for a in range(2):
            for mask in final:
                guarded([place(k)[1]], lambda a=a, mask=mask, k=k: column_arrival(a, mask, k).wait_recv())
    for s in range(1, n_dp):
        for kind in range(2):
            weight_copy(kind, s).wait_send()
            for h in range(1, n_groups):
                share_arrival(kind, s, h).wait_recv()
                share_copy(kind, s, h).wait_send()
    for a in range(2):
        for side in range(2):
            for s in range(1, n_dp):
                guarded(
                    line_send_conditions(side, s),
                    lambda a=a, side=side, s=s: line_copy(a, side, s).wait_send(),
                )
        for mask in [0] + through:
            for k in order:
                for bit in next_bits(mask):
                    guarded(
                        [place(k)[1]],
                        lambda a=a, mask=mask, k=k, bit=bit: column_copy(a, mask, k, bit).wait_send(),
                    )
    for copy in local:
        copy.wait()


def scatter_kernel(
    n_groups, n_tensor, n_dp, grad_scale,
    branch_ref, back_ref, g_up_ref, g_down_ref, first_ref, second_ref, grad_ref, gain_ref,
    second_in_ref, grad_first_ref, grad_norm_ref, up_out, down_out,
    fold, right, left, stat_line, stat_fold, local_sem,
    fold_send, fold_recv, line_send, line_recv, grads_send, grads_recv,
    stat_send, stat_recv, pair_send, pair_recv,
):
    group, tensor, dp = (lax.axis_index(name) for name in ("groups", "tensor", "dp"))
    bits = n_tensor.bit_length() - 1
    rows, width = first_ref.shape
    units = g_up_ref.shape[1]
    depth = g_up_ref.shape[0] // n_dp
    partials = (branch_ref, back_ref)
    fold_sems, line_sems = (fold_send, fold_recv), (line_send, line_recv)
    grads_sems, stat_sems, pair_sems = (
        (grads_send, grads_recv), (stat_send, stat_recv), (pair_send, pair_recv),
    )
    slots = {}
    for bit in range(bits):
        for mask in range(0, n_tensor, 2 << bit):
            slots[bit, mask] = len(slots)

    def grads_copy(kind, s):
        target = (dp + s) % n_dp
        if kind == 0:
            src, dst = g_up_ref.at[span(target, depth), :], up_out.at[:, span(dp, units)]
        else:
            src, dst = g_down_ref.at[:, span(target, depth)], down_out.at[span(dp, units), :]
        return remote(src, dst, grads_sems, (kind, s), {"dp": target})

    def grads_arrival(kind, s):
        source = (dp + n_dp - s) % n_dp
        here = up_out.at[:, span(source, units)] if kind == 0 else down_out.at[span(source, units), :]
        return remote(here, here, grads_sems, (kind, s), {"dp": (dp + s) % n_dp})

    def current(a, bit, mask, b):
        if bit == 0:
            return partials[a].at[span(flipped(tensor, mask, bits) * n_dp + b, rows), :]
        return fold.at[a, slots[bit - 1, mask], b]

    def fold_copy(a, bit, mask, b):
        slot = slots[bit, mask ^ 1 << bit]
        return remote(
            current(a, bit, mask, b), fold.at[a, slot, b], fold_sems, (a, slot, b),
            {"tensor": flipped(tensor, 1 << bit, bits)},
        )

    def fold_arrival(a, bit, mask, b):
        slot = slots[bit, mask]
        here = fold.at[a, slot, b]
        return remote(
            here, here, fold_sems, (a, slot, b), {"tensor": flipped(tensor, 1 << bit, bits)}
        )

    def add_into(ref, other):
        @pl.loop(0, rows // 16)
        def _(i):
            cut = pl.ds(pl.multiple_of(i * 16, 16), 16)
            ref[cut, :] = (
                ref[cut, :].astype(jnp.float32) + other[cut, :].astype(jnp.float32)
            ).astype(ref.dtype)

    greet(n_groups, n_dp, bits, group, tensor, dp)

    def sent_masks(bit):
        masks = [m for m in range(n_tensor) if m % (1 << bit) == 0 and m >> bit & 1]
        return sorted(masks, reverse=True)

    def kept_masks(bit):
        return sorted(range(0, n_tensor, 2 << bit), reverse=True)

    for mask in sent_masks(0):
        for b in range(n_dp):
            for a in range(2):
                fold_copy(a, 0, mask, b).start()
    for s in range(1, n_dp):
        for kind in range(2):
            grads_copy(kind, s).start()
    local = [
        pltpu.make_async_copy(
            g_up_ref.at[span(dp, depth), :], up_out.at[:, span(dp, units)], local_sem.at[0]
        ),
        pltpu.make_async_copy(
            g_down_ref.at[:, span(dp, depth)], down_out.at[span(dp, units), :], local_sem.at[1]
        ),
    ]
    for copy in local:
        copy.start()
    for bit in range(bits):
        for mask in kept_masks(bit):
            for b in range(n_dp):
                for a in range(2):
                    fold_arrival(a, bit, mask, b).wait_recv()
                    add_into(fold.at[a, slots[bit, mask], b], current(a, bit, mask, b))
                    if bit + 1 < bits and mask in sent_masks(bit + 1):
                        fold_copy(a, bit + 1, mask, b).start()

    last = slots[bits - 1, 0]
    moving = (right, left)

    def line_conditions(side, s):
        return dp + s <= n_dp - 1 if side == 0 else dp >= s

    def behind(side):
        return dp >= 1 if side == 0 else dp <= n_dp - 2

    def line_peer(side):
        return {"dp": (dp + 1) % n_dp if side == 0 else (dp + n_dp - 1) % n_dp}

    def line_copy(a, side, s, relayed):
        target = dp + s if side == 0 else dp - s
        src = moving[side].at[a, s] if relayed else fold.at[a, last, target]
        return remote(src, moving[side].at[a, s - 1], line_sems, (a, side, s - 1), line_peer(side))

    def line_arrival(a, side, s):
        here = moving[side].at[a, s]
        return remote(here, here, line_sems, (a, side, s), line_peer(side))

    for s in range(n_dp - 1, 0, -1):
        for a in range(2):
            for side in range(2):
                @pl.when(jnp.logical_and(line_conditions(side, s), jnp.logical_not(behind(side))))
                def _(a=a, side=side, s=s):
                    line_copy(a, side, s, False).start()

                if s <= n_dp - 2:
                    @pl.when(jnp.logical_and(line_conditions(side, s), behind(side)))
                    def _(a=a, side=side, s=s):
                        target = dp + s if side == 0 else dp - s
                        line_arrival(a, side, s).wait_recv()
                        add_into(moving[side].at[a, s], fold.at[a, last, target])
                        line_copy(a, side, s, True).start()

    for a in range(2):
        for side in range(2):
            @pl.when(behind(side))
            def _(a=a, side=side):
                line_arrival(a, side, 0).wait_recv()

            @pl.when(jnp.logical_not(behind(side)))
            def _(a=a, side=side):
                moving[side][a, 0] = jnp.zeros((rows, width), moving[side].dtype)

    stat_line[dp] = jnp.zeros(stat_line.shape[1:], jnp.float32)

    @pl.loop(0, rows // 16)
    def _(i):
        cut = pl.ds(pl.multiple_of(i * 16, 16), 16)

        def total(a):
            return (
                fold[a, last, dp, cut, :].astype(jnp.float32)
                + right[a, 0, cut, :].astype(jnp.float32)
                + left[a, 0, cut, :].astype(jnp.float32)
            )

        second_in_ref[cut, :] = (second_ref[cut, :].astype(jnp.float32) - total(0)).astype(
            second_in_ref.dtype
        )
        standard, inv_std = standardize(first_ref[cut, :])
        grad_normed = total(1)
        stat_line[dp, 0:1, :] += jnp.sum(grad_normed * standard, axis=0, keepdims=True)
        stat_line[dp, 1:2, :] += jnp.sum(grad_normed, axis=0, keepdims=True)
        grad_std = grad_normed * gain_ref[...]
        grad_rows = inv_std * (
            grad_std
            - jnp.mean(grad_std, axis=-1, keepdims=True)
            - standard * jnp.mean(grad_std * standard, axis=-1, keepdims=True)
        )
        grad_first_ref[cut, :] = grad_ref[cut, :].astype(jnp.float32) + grad_rows

    def stat_copy(s):
        here = stat_line.at[dp]
        return remote(here, here, stat_sems, s, {"dp": (dp + s) % n_dp})

    def stat_arrival(s):
        here = stat_line.at[(dp + n_dp - s) % n_dp]
        return remote(here, here, stat_sems, s, {"dp": (dp + s) % n_dp})

    for s in range(1, n_dp):
        stat_copy(s).start()
    for s in range(1, n_dp):
        stat_arrival(s).wait_recv()
    sums = stat_line[0]
    for source in range(1, n_dp):
        sums = sums + stat_line[source]
    for bit in range(bits):
        stat_fold[bit, 0] = sums
        copy = remote(
            stat_fold.at[bit, 0], stat_fold.at[bit, 1], pair_sems, bit,
            {"tensor": flipped(tensor, 1 << bit, bits)},
        )
        copy.start()
        copy.wait()
        sums = stat_fold[bit, 0] + stat_fold[bit, 1]
    grad_norm_ref[...] = sums[0:2] * grad_scale

    for s in range(1, n_dp):
        stat_copy(s).wait_send()
        for kind in range(2):
            grads_arrival(kind, s).wait_recv()
            grads_copy(kind, s).wait_send()
    for copy in local:
        copy.wait()
    for bit in range(bits):
        for mask in sent_masks(bit):
            for b in range(n_dp):
                for a in range(2):
                    fold_copy(a, bit, mask, b).wait_send()
    for s in range(n_dp - 1, 0, -1):
        for a in range(2):
            for side in range(2):
                @pl.when(line_conditions(side, s))
                def _(a=a, side=side, s=s):
                    line_copy(a, side, s, s <= n_dp - 2).wait_send()


def standardize(row_data):
    values = row_data.astype(jnp.float32)
    centred = values - jnp.mean(values, axis=-1, keepdims=True)
    inv_std = lax.rsqrt(jnp.mean(centred * centred, axis=-1, keepdims=True) + epsilon)
    return centred * inv_std, inv_std


ANY = pl.BlockSpec(memory_space=pl.ANY)
VMEM = pl.BlockSpec(memory_space=pltpu.VMEM)
DMA = pltpu.SemaphoreType.DMA


def spread_body(sizes, first_out, second_out, grad_first, grad_second, w_up, w_down, norm_gain, norm_bias):
    n_groups, n_tensor, n_dp = sizes
    rows, width = first_out.shape
    tokens = rows * n_tensor * n_dp
    units = w_up.shape[1] // n_dp
    bits = n_tensor.bit_length() - 1
    half = jnp.bfloat16
    grad_scale = tokens ** (-0.5)
    _, _, own_normed = normalize(first_out, norm_gain, norm_bias)
    normed, grad_all, up, down = pl.pallas_call(
        functools.partial(gather_kernel, n_groups, n_tensor, n_dp),
        out_shape=(
            jax.ShapeDtypeStruct((tokens, width), half),
            jax.ShapeDtypeStruct((tokens, width), half),
            jax.ShapeDtypeStruct((width, units), half),
            jax.ShapeDtypeStruct((units, width), half),
        ),
        in_specs=[VMEM] * 4,
        out_specs=(ANY,) * 4,
        scratch_shapes=[DMA((4,))]
        + [DMA((2, 2, n_dp))] * 2
        + [DMA((2, n_tensor, 2 * n_dp - 1))] * 2
        + [DMA((2, n_dp))] * 2
        + [DMA((2, n_dp, n_groups))] * 2,
        compiler_params=pltpu.CompilerParams(collective_id=0, has_side_effects=True),
        name="gather_all",
    )(own_normed, grad_second, w_up, w_down)

    preact = jnp.dot(normed, up, preferred_element_type=jnp.float32)
    hidden = jax.nn.gelu(preact).astype(half)
    grad_hidden = lax.dot_general(
        grad_all, down, (((1,), (1,)), ((), ())), preferred_element_type=jnp.float32
    )
    grad_pre = jax.vjp(jax.nn.gelu, preact)[1](grad_hidden)[0].astype(half)
    branch = jnp.dot(hidden, down, preferred_element_type=jnp.float32).astype(half)
    back = lax.dot_general(
        grad_pre, up, (((1,), (1,)), ((), ())), preferred_element_type=jnp.float32
    ).astype(half)
    g_down = contract_tokens(hidden, grad_all).astype(half)
    g_up = contract_tokens(normed, grad_pre).astype(half)

    second_in, grad_first_in, grad_norm, up_out, down_out = pl.pallas_call(
        functools.partial(scatter_kernel, n_groups, n_tensor, n_dp, grad_scale),
        out_shape=(
            jax.ShapeDtypeStruct((rows, width), half),
            jax.ShapeDtypeStruct((rows, width), jnp.float32),
            jax.ShapeDtypeStruct((2, width), jnp.float32),
            jax.ShapeDtypeStruct((w_up.shape[0], w_up.shape[1]), half),
            jax.ShapeDtypeStruct((w_down.shape[0], w_down.shape[1]), half),
        ),
        in_specs=[VMEM] * 8,
        out_specs=(VMEM,) * 3 + (ANY,) * 2,
        scratch_shapes=[
            pltpu.VMEM((2, n_tensor - 1, n_dp, rows, width), half),
            pltpu.VMEM((2, n_dp - 1, rows, width), half),
            pltpu.VMEM((2, n_dp - 1, rows, width), half),
            pltpu.VMEM((n_dp, 8, width), jnp.float32),
            pltpu.VMEM((bits, 2, 8, width), jnp.float32),
            DMA((2,)),
        ]
        + [DMA((2, n_tensor - 1, n_dp))] * 2
        + [DMA((2, 2, n_dp - 1))] * 2
        + [DMA((2, n_dp))] * 2
        + [DMA((n_dp,))] * 2
        + [DMA((bits,))] * 2,
        compiler_params=pltpu.CompilerParams(collective_id=1, has_side_effects=True),
        name="scatter_all",
    )(branch, back, g_up, g_down, first_out, second_out, grad_first, norm_gain.reshape(1, -1))
    grad_up = up_out.astype(jnp.float32) * grad_scale
    grad_down = down_out.astype(jnp.float32) * grad_scale
    return second_in, grad_first_in, grad_up, grad_down, grad_norm


def choose(sizes, *args):
    first_out, w_up = args[0], args[4]
    n_groups, n_tensor, n_dp = sizes
    tokens = first_out.shape[0] * n_tensor * n_dp
    fits = (
        n_tensor > 1
        and n_dp > 1
        and n_tensor & (n_tensor - 1) == 0
        and w_up.shape[1] % (n_dp * n_groups * 128) == 0
        and w_up.shape[0] % (n_groups * 128) == 0
    )
    if fits and tokens <= w_up.shape[1]:
        return spread_body(sizes, *args)
    return body(*args)


def solution(mesh):
    in_specs = (
        P(("groups", "tensor", "dp"), None),
        P(("groups", "tensor", "dp"), None),
        P(("groups", "tensor", "dp"), None),
        P(("groups", "tensor", "dp"), None),
        P("dp", "tensor"),
        P("tensor", "dp"),
        P(),
        P(),
    )
    out_specs = (
        P(("groups", "tensor", "dp"), None),
        P(("groups", "tensor", "dp"), None),
        P(("groups", "dp"), "tensor"),
        P(("groups", "tensor"), "dp"),
        P("groups", None),
    )
    sizes = tuple(mesh.shape[name] for name in ("groups", "tensor", "dp"))
    return jax.shard_map(functools.partial(choose, sizes), mesh=mesh, in_specs=in_specs, out_specs=out_specs, check_vma=False)
```

```python
import functools

import jax
import jax.numpy as jnp
from jax import lax
from jax.experimental import pallas as pl
from jax.experimental.pallas import tpu as pltpu
from jax.sharding import PartitionSpec as P

epsilon = 1e-06


def normalize(row_data, norm_gain, norm_bias):
    values = row_data.astype(jnp.float32)
    row_mean = jnp.mean(values, axis=-1, keepdims=True)
    centred = values - row_mean
    inv_std = lax.rsqrt(jnp.mean(centred * centred, axis=-1, keepdims=True) + epsilon)
    standard = centred * inv_std
    normed = (standard * norm_gain + norm_bias).astype(jnp.bfloat16)
    return (standard, inv_std, normed)


def contract_tokens(left_rows, right_rows):
    return lax.dot_general(
        left_rows, right_rows, (((0,), (0,)), ((), ())), preferred_element_type=jnp.float32
    )


def body(first_out, second_out, grad_first, grad_second, w_up, w_down, norm_gain, norm_bias):
    own_rows = first_out.shape[0]
    up_full, down_full = (
        lax.all_gather(w_up, "dp", axis=0, tiled=True),
        lax.all_gather(w_down, "dp", axis=1, tiled=True),
    )
    first_all, grad_all = (
        lax.all_gather(first_out, "tensor", axis=0, tiled=True),
        lax.all_gather(grad_second, "tensor", axis=0, tiled=True),
    )
    standard_all, inv_std_all, normed = normalize(first_all, norm_gain, norm_bias)
    offset = lax.axis_index("tensor") * own_rows
    standard = lax.dynamic_slice_in_dim(standard_all, offset, own_rows, 0)
    inv_std = lax.dynamic_slice_in_dim(inv_std_all, offset, own_rows, 0)
    preact = jnp.dot(normed, up_full, preferred_element_type=jnp.float32)
    hidden = jax.nn.gelu(preact).astype(jnp.bfloat16)
    branch = lax.psum_scatter(
        jnp.dot(hidden, down_full, preferred_element_type=jnp.float32).astype(jnp.bfloat16),
        "tensor",
        scatter_dimension=0,
        tiled=True,
    ).astype(jnp.float32)
    second_in = (second_out.astype(jnp.float32) - branch).astype(jnp.bfloat16)
    tokens = own_rows * lax.axis_size("tensor") * lax.axis_size("dp")
    grad_scale = tokens ** (-0.5)
    grad_down_part = contract_tokens(hidden, grad_all)
    grad_down = (
        lax.psum_scatter(
            grad_down_part.astype(jnp.bfloat16), "dp", scatter_dimension=1, tiled=True
        ).astype(jnp.float32)
        * grad_scale
    )
    grad_hidden = lax.dot_general(
        grad_all, down_full, (((1,), (1,)), ((), ())), preferred_element_type=jnp.float32
    )
    grad_pre = jax.vjp(jax.nn.gelu, preact)[1](grad_hidden)[0].astype(jnp.bfloat16)
    grad_up_part = contract_tokens(normed, grad_pre)
    grad_up = (
        lax.psum_scatter(
            grad_up_part.astype(jnp.bfloat16), "dp", scatter_dimension=0, tiled=True
        ).astype(jnp.float32)
        * grad_scale
    )
    grad_normed = lax.psum_scatter(
        lax.dot_general(
            grad_pre, up_full, (((1,), (1,)), ((), ())), preferred_element_type=jnp.float32
        ).astype(jnp.bfloat16),
        "tensor",
        scatter_dimension=0,
        tiled=True,
    ).astype(jnp.float32)
    grad_std = grad_normed * norm_gain
    grad_rows = inv_std * (
        grad_std
        - jnp.mean(grad_std, axis=-1, keepdims=True)
        - standard * jnp.mean(grad_std * standard, axis=-1, keepdims=True)
    )
    grad_first_in = grad_first.astype(jnp.float32) + grad_rows
    local_stats = jnp.stack([jnp.sum(grad_normed * standard, axis=0), jnp.sum(grad_normed, axis=0)])
    grad_norm = lax.psum(local_stats, ("tensor", "dp")) * grad_scale
    return (second_in, grad_first_in, grad_up, grad_down, grad_norm)


def span(index, size):
    return pl.ds(pl.multiple_of(index * size, size), size)


def flipped(index, mask, bits):
    for bit in range(bits):
        if mask >> bit & 1:
            step = 1 << bit
            index = index + (1 - 2 * ((index // step) % 2)) * step
    return index


def greet(n_groups, n_dp, bits, group, tensor, dp):
    barrier = pltpu.get_barrier_semaphore()
    peers = [{"dp": (dp + s) % n_dp} for s in range(1, n_dp)]
    peers += [{"tensor": flipped(tensor, 1 << bit, bits)} for bit in range(bits)]
    peers += [{"groups": (group + s) % n_groups} for s in range(1, n_groups)]
    for peer in peers:
        pl.semaphore_signal(
            barrier, inc=1, device_id=peer, device_id_type=pl.DeviceIdType.MESH
        )
    pl.semaphore_wait(barrier, len(peers))


def remote(src, dst, sems, index, peer):
    return pltpu.make_async_remote_copy(
        src_ref=src,
        dst_ref=dst,
        send_sem=sems[0].at[index],
        recv_sem=sems[1].at[index],
        device_id=peer,
        device_id_type=pl.DeviceIdType.MESH,
    )


def gather_kernel(
    n_groups, n_tensor, n_dp,
    first_ref, grad_ref, w_up_ref, w_down_ref, gain_ref, bias_ref,
    normed_all, grad_all, up_ref, down_ref,
    own_normed, local_sem, line_send, line_recv, column_send, column_recv,
    weight_send, weight_recv, share_send, share_recv,
):
    group, tensor, dp = (lax.axis_index(name) for name in ("groups", "tensor", "dp"))
    bits = n_tensor.bit_length() - 1
    rows = first_ref.shape[0]
    depth = w_up_ref.shape[0]
    units = w_up_ref.shape[1] // n_dp
    outputs = (normed_all, grad_all)
    line_sems, column_sems = (line_send, line_recv), (column_send, column_recv)
    weight_sems, share_sems = (weight_send, weight_recv), (share_send, share_recv)

    def block(a, mask, source):
        return outputs[a].at[span(flipped(tensor, mask, bits) * n_dp + source, rows), :]

    def place(k):
        if k == 0:
            return dp, None
        if k < n_dp:
            return dp - k, dp >= k
        return dp + (k - n_dp + 1), dp + (k - n_dp + 1) <= n_dp - 1

    def guarded(conditions, action):
        conditions = [c for c in conditions if c is not None]
        if not conditions:
            action()
        else:
            pl.when(functools.reduce(jnp.logical_and, conditions))(action)

    def line_copy(a, side, distance):
        if side == 0:
            source, target = dp - (distance - 1), dp + 1
        else:
            source, target = dp + (distance - 1), dp - 1
        src = grad_ref if a == 1 and distance == 1 else block(a, 0, source)
        return remote(src, block(a, 0, source), line_sems, (a, side, distance), {"dp": target})

    def line_send_conditions(side, distance):
        if side == 0:
            return [dp >= distance - 1 if distance > 1 else None, dp <= n_dp - 2]
        return [dp <= n_dp - distance if distance > 1 else None, dp >= 1]

    def column_copy(a, mask, k, bit):
        source, _ = place(k)
        src = grad_ref if a == 1 and mask == 0 and k == 0 else block(a, mask, source)
        return remote(
            src, block(a, mask, source), column_sems, (a, mask | 1 << bit, k),
            {"tensor": flipped(tensor, 1 << bit, bits)},
        )

    def column_arrival(a, mask, k):
        source, _ = place(k)
        bit = (mask & -mask).bit_length() - 1
        here = block(a, mask, source)
        return remote(
            here, here, column_sems, (a, mask, k), {"tensor": flipped(tensor, 1 << bit, bits)}
        )

    def next_bits(mask):
        top = bits if mask == 0 else (mask & -mask).bit_length() - 1
        return list(reversed(range(top)))

    def pass_on(a, mask, k):
        for bit in next_bits(mask):
            column_copy(a, mask, k, bit).start()

    part = depth // n_groups
    piece = units // n_groups

    def weight_views(kind, source, owner):
        if kind == 0:
            return up_ref.at[span(source * n_groups + owner, part), :]
        return down_ref.at[span(owner, piece), span(source, depth)]

    def weight_copy(kind, s):
        target = (dp + s) % n_dp
        if kind == 0:
            src = w_up_ref.at[span(group, part), span(target, units)]
        else:
            src = w_down_ref.at[span(target * n_groups + group, piece), :]
        return remote(src, weight_views(kind, dp, group), weight_sems, (kind, s), {"dp": target})

    def weight_arrival(kind, s):
        here = weight_views(kind, (dp + n_dp - s) % n_dp, group)
        return remote(here, here, weight_sems, (kind, s), {"dp": (dp + s) % n_dp})

    def share_copy(kind, s, h):
        here = weight_views(kind, (dp + n_dp - s) % n_dp, group)
        return remote(here, here, share_sems, (kind, s, h), {"groups": (group + h) % n_groups})

    def share_arrival(kind, s, h):
        here = weight_views(kind, (dp + n_dp - s) % n_dp, (group + n_groups - h) % n_groups)
        return remote(here, here, share_sems, (kind, s, h), {"groups": (group + h) % n_groups})

    greet(n_groups, n_dp, bits, group, tensor, dp)
    order = [0] + [k for s in range(1, n_dp) for k in (s, s + n_dp - 1)]
    def send_own(a):
        for side in range(2):
            guarded(
                line_send_conditions(side, 1), lambda side=side: line_copy(a, side, 1).start()
            )
        pass_on(a, 0, 0)

    send_own(1)
    for s in range(1, n_dp):
        for kind in range(2):
            weight_copy(kind, s).start()
    local = [
        pltpu.make_async_copy(grad_ref, block(1, 0, dp), local_sem.at[1]),
        pltpu.make_async_copy(
            w_up_ref.at[:, span(dp, units)], up_ref.at[span(dp, depth), :], local_sem.at[2]
        ),
        pltpu.make_async_copy(
            w_down_ref.at[span(dp, units), :], down_ref.at[:, span(dp, depth)], local_sem.at[3]
        ),
    ]
    for copy in local:
        copy.start()

    @pl.loop(0, rows // 16)
    def _(i):
        cut = pl.ds(pl.multiple_of(i * 16, 16), 16)
        standard, _ = standardize(first_ref[cut, :])
        own_normed[cut, :] = (standard * gain_ref[...] + bias_ref[...]).astype(own_normed.dtype)

    settle = pltpu.make_async_copy(own_normed, block(0, 0, dp), local_sem.at[0])
    settle.start()
    settle.wait()
    send_own(0)

    through = [m for m in range(1, n_tensor) if next_bits(m)]
    final = [m for m in range(1, n_tensor) if not next_bits(m)]

    def relay(k):
        for a in range(2):
            for mask in sorted(through, reverse=True):
                def action(a=a, mask=mask):
                    column_arrival(a, mask, k).wait_recv()
                    pass_on(a, mask, k)
                guarded([place(k)[1]], action)

    done = [[0]] + [[s, s + n_dp - 1] for s in range(1, n_dp)]
    for s in range(1, n_dp):
        for a in range(2):
            for side in range(2):
                k = done[s][side]

                def action(a=a, side=side, k=k, s=s):
                    source, _ = place(k)
                    here = block(a, 0, source)
                    remote(here, here, line_sems, (a, side, s), {"dp": (dp + 1) % n_dp}).wait_recv()
                    if s < n_dp - 1:
                        guarded(
                            line_send_conditions(side, s + 1),
                            lambda: line_copy(a, side, s + 1).start(),
                        )
                    pass_on(a, 0, k)

                guarded([place(k)[1]], action)
        for k in done[s - 1]:
            relay(k)
        for kind in range(2):
            weight_arrival(kind, s).wait_recv()
            for h in range(1, n_groups):
                share_copy(kind, s, h).start()
    for k in done[n_dp - 1]:
        relay(k)
    for k in order:
        for a in range(2):
            for mask in final:
                guarded([place(k)[1]], lambda a=a, mask=mask, k=k: column_arrival(a, mask, k).wait_recv())
    for s in range(1, n_dp):
        for kind in range(2):
            weight_copy(kind, s).wait_send()
            for h in range(1, n_groups):
                share_arrival(kind, s, h).wait_recv()
                share_copy(kind, s, h).wait_send()
    for a in range(2):
        for side in range(2):
            for s in range(1, n_dp):
                guarded(
                    line_send_conditions(side, s),
                    lambda a=a, side=side, s=s: line_copy(a, side, s).wait_send(),
                )
        for mask in [0] + through:
            for k in order:
                for bit in next_bits(mask):
                    guarded(
                        [place(k)[1]],
                        lambda a=a, mask=mask, k=k, bit=bit: column_copy(a, mask, k, bit).wait_send(),
                    )
    for copy in local:
        copy.wait()


def scatter_kernel(
    n_groups, n_tensor, n_dp, grad_scale,
    hidden_ref, pre_ref, up_ref, down_ref, g_up_ref, g_down_ref,
    first_ref, second_ref, grad_ref, gain_ref,
    second_in_ref, grad_first_ref, grad_norm_ref, up_out, down_out,
    partials, fold, right, left, stat_line, stat_fold, local_sem,
    fold_send, fold_recv, line_send, line_recv, grads_send, grads_recv,
    stat_send, stat_recv, pair_send, pair_recv,
):
    group, tensor, dp = (lax.axis_index(name) for name in ("groups", "tensor", "dp"))
    bits = n_tensor.bit_length() - 1
    rows, width = first_ref.shape
    units = g_up_ref.shape[1]
    depth = g_up_ref.shape[0] // n_dp
    fold_sems, line_sems = (fold_send, fold_recv), (line_send, line_recv)
    grads_sems, stat_sems, pair_sems = (
        (grads_send, grads_recv), (stat_send, stat_recv), (pair_send, pair_recv),
    )
    slots = {}
    for bit in range(bits):
        for mask in range(0, n_tensor, 2 << bit):
            slots[bit, mask] = len(slots)

    def grads_copy(kind, s):
        target = (dp + s) % n_dp
        if kind == 0:
            src, dst = g_up_ref.at[span(target, depth), :], up_out.at[:, span(dp, units)]
        else:
            src, dst = g_down_ref.at[:, span(target, depth)], down_out.at[span(dp, units), :]
        return remote(src, dst, grads_sems, (kind, s), {"dp": target})

    def grads_arrival(kind, s):
        source = (dp + n_dp - s) % n_dp
        here = up_out.at[:, span(source, units)] if kind == 0 else down_out.at[span(source, units), :]
        return remote(here, here, grads_sems, (kind, s), {"dp": (dp + s) % n_dp})

    def current(a, bit, mask, b):
        if bit == 0:
            return partials.at[a, mask, b]
        return fold.at[a, slots[bit - 1, mask], b]

    def fold_copy(a, bit, mask, b):
        slot = slots[bit, mask ^ 1 << bit]
        return remote(
            current(a, bit, mask, b), fold.at[a, slot, b], fold_sems, (a, slot, b),
            {"tensor": flipped(tensor, 1 << bit, bits)},
        )

    def fold_arrival(a, bit, mask, b):
        slot = slots[bit, mask]
        here = fold.at[a, slot, b]
        return remote(
            here, here, fold_sems, (a, slot, b), {"tensor": flipped(tensor, 1 << bit, bits)}
        )

    def add_into(ref, other):
        @pl.loop(0, rows // 16)
        def _(i):
            cut = pl.ds(pl.multiple_of(i * 16, 16), 16)
            ref[cut, :] = (
                ref[cut, :].astype(jnp.float32) + other[cut, :].astype(jnp.float32)
            ).astype(ref.dtype)

    greet(n_groups, n_dp, bits, group, tensor, dp)

    def sent_masks(bit):
        masks = [m for m in range(n_tensor) if m % (1 << bit) == 0 and m >> bit & 1]
        return sorted(masks, reverse=True)

    def kept_masks(bit):
        return sorted(range(0, n_tensor, 2 << bit), reverse=True)

    for s in range(1, n_dp):
        grads_copy(0, s).start()
    local = [
        pltpu.make_async_copy(
            g_up_ref.at[span(dp, depth), :], up_out.at[:, span(dp, units)], local_sem.at[0]
        ),
        pltpu.make_async_copy(
            g_down_ref.at[:, span(dp, depth)], down_out.at[span(dp, units), :], local_sem.at[1]
        ),
    ]
    for copy in local:
        copy.start()

    way = 2 * ((2 * dp) // n_dp) - 1

    def multiply(mask, b):
        cut = span(flipped(tensor, mask, bits) * n_dp + b, rows)
        partials[0, mask, b] = jnp.dot(
            hidden_ref[cut, :], down_ref[...], preferred_element_type=jnp.float32
        ).astype(partials.dtype)
        partials[1, mask, b] = lax.dot_general(
            pre_ref[cut, :], up_ref[...], (((1,), (1,)), ((), ())),
            preferred_element_type=jnp.float32,
        ).astype(partials.dtype)

    def folded(bit, mask, b):
        for a in range(2):
            fold_arrival(a, bit, mask, b).wait_recv()
            add_into(fold.at[a, slots[bit, mask], b], current(a, bit, mask, b))
            if bit + 1 < bits and mask in sent_masks(bit + 1):
                fold_copy(a, bit + 1, mask, b).start()

    for mask in sent_masks(0):
        @pl.loop(0, n_dp)
        def _(i, mask=mask):
            b = (dp + way * (1 + i) + n_dp) % n_dp
            multiply(mask, b)
            for a in range(2):
                fold_copy(a, 0, mask, b).start()

        @pl.loop(0, n_dp)
        def _(i, mask=mask):
            b = (dp + way * (1 + i) + n_dp) % n_dp
            multiply(mask - 1, b)
            folded(0, mask - 1, b)

    for bit in range(1, bits - 1):
        for mask in kept_masks(bit):
            for i in range(n_dp):
                folded(bit, mask, (dp + way * (1 + i) + n_dp) % n_dp)

    def finish(b):
        if bits > 1:
            folded(bits - 1, 0, b)

    last = slots[bits - 1, 0]
    moving = (right, left)

    def line_conditions(side, s):
        return dp + s <= n_dp - 1 if side == 0 else dp >= s

    def behind(side):
        return dp >= 1 if side == 0 else dp <= n_dp - 2

    def line_peer(side):
        return {"dp": (dp + 1) % n_dp if side == 0 else (dp + n_dp - 1) % n_dp}

    def line_copy(a, side, s, relayed):
        target = dp + s if side == 0 else dp - s
        src = moving[side].at[a, s] if relayed else fold.at[a, last, target]
        return remote(src, moving[side].at[a, s - 1], line_sems, (a, side, s - 1), line_peer(side))

    def line_arrival(a, side, s):
        here = moving[side].at[a, s]
        return remote(here, here, line_sems, (a, side, s), line_peer(side))

    for s in range(n_dp - 1, 0, -1):
        for side in range(2):
            @pl.when(jnp.logical_and(line_conditions(side, s), jnp.logical_not(behind(side))))
            def _(side=side, s=s):
                finish(dp + s if side == 0 else dp - s)
                for a in range(2):
                    line_copy(a, side, s, False).start()

            if s <= n_dp - 2:
                @pl.when(jnp.logical_and(line_conditions(side, s), behind(side)))
                def _(side=side, s=s):
                    target = dp + s if side == 0 else dp - s
                    finish(target)
                    for a in range(2):
                        line_arrival(a, side, s).wait_recv()
                        add_into(moving[side].at[a, s], fold.at[a, last, target])
                        line_copy(a, side, s, True).start()
        grads_copy(1, s).start()
    finish(dp)

    for a in range(2):
        for side in range(2):
            @pl.when(behind(side))
            def _(a=a, side=side):
                line_arrival(a, side, 0).wait_recv()

            @pl.when(jnp.logical_not(behind(side)))
            def _(a=a, side=side):
                moving[side][a, 0] = jnp.zeros((rows, width), moving[side].dtype)

    stat_line[dp] = jnp.zeros(stat_line.shape[1:], jnp.float32)

    @pl.loop(0, rows // 16)
    def _(i):
        cut = pl.ds(pl.multiple_of(i * 16, 16), 16)

        def total(a):
            return (
                fold[a, last, dp, cut, :].astype(jnp.float32)
                + right[a, 0, cut, :].astype(jnp.float32)
                + left[a, 0, cut, :].astype(jnp.float32)
            )

        second_in_ref[cut, :] = (second_ref[cut, :].astype(jnp.float32) - total(0)).astype(
            second_in_ref.dtype
        )
        standard, inv_std = standardize(first_ref[cut, :])
        grad_normed = total(1)
        stat_line[dp, 0:1, :] += jnp.sum(grad_normed * standard, axis=0, keepdims=True)
        stat_line[dp, 1:2, :] += jnp.sum(grad_normed, axis=0, keepdims=True)
        grad_std = grad_normed * gain_ref[...]
        grad_rows = inv_std * (
            grad_std
            - jnp.mean(grad_std, axis=-1, keepdims=True)
            - standard * jnp.mean(grad_std * standard, axis=-1, keepdims=True)
        )
        grad_first_ref[cut, :] = grad_ref[cut, :].astype(jnp.float32) + grad_rows

    def stat_copy(s):
        here = stat_line.at[dp]
        return remote(here, here, stat_sems, s, {"dp": (dp + s) % n_dp})

    def stat_arrival(s):
        here = stat_line.at[(dp + n_dp - s) % n_dp]
        return remote(here, here, stat_sems, s, {"dp": (dp + s) % n_dp})

    for s in range(1, n_dp):
        stat_copy(s).start()
    for s in range(1, n_dp):
        stat_arrival(s).wait_recv()
    sums = stat_line[0]
    for source in range(1, n_dp):
        sums = sums + stat_line[source]
    for bit in range(bits):
        stat_fold[bit, 0] = sums
        copy = remote(
            stat_fold.at[bit, 0], stat_fold.at[bit, 1], pair_sems, bit,
            {"tensor": flipped(tensor, 1 << bit, bits)},
        )
        copy.start()
        copy.wait()
        sums = stat_fold[bit, 0] + stat_fold[bit, 1]
    grad_norm_ref[...] = sums[0:2] * grad_scale

    for s in range(1, n_dp):
        stat_copy(s).wait_send()
        for kind in range(2):
            grads_arrival(kind, s).wait_recv()
            grads_copy(kind, s).wait_send()
    for copy in local:
        copy.wait()
    for bit in range(bits):
        for mask in sent_masks(bit):
            for b in range(n_dp):
                for a in range(2):
                    fold_copy(a, bit, mask, b).wait_send()
    for s in range(n_dp - 1, 0, -1):
        for a in range(2):
            for side in range(2):
                @pl.when(line_conditions(side, s))
                def _(a=a, side=side, s=s):
                    line_copy(a, side, s, s <= n_dp - 2).wait_send()


def standardize(row_data):
    values = row_data.astype(jnp.float32)
    centred = values - jnp.mean(values, axis=-1, keepdims=True)
    inv_std = lax.rsqrt(jnp.mean(centred * centred, axis=-1, keepdims=True) + epsilon)
    return centred * inv_std, inv_std


ANY = pl.BlockSpec(memory_space=pl.ANY)
VMEM = pl.BlockSpec(memory_space=pltpu.VMEM)
DMA = pltpu.SemaphoreType.DMA


def spread_body(sizes, first_out, second_out, grad_first, grad_second, w_up, w_down, norm_gain, norm_bias):
    n_groups, n_tensor, n_dp = sizes
    rows, width = first_out.shape
    tokens = rows * n_tensor * n_dp
    units = w_up.shape[1] // n_dp
    bits = n_tensor.bit_length() - 1
    half = jnp.bfloat16
    grad_scale = tokens ** (-0.5)
    gain, bias = norm_gain.reshape(1, -1), norm_bias.reshape(1, -1)
    normed, grad_all, up, down = pl.pallas_call(
        functools.partial(gather_kernel, n_groups, n_tensor, n_dp),
        out_shape=(
            jax.ShapeDtypeStruct((tokens, width), half),
            jax.ShapeDtypeStruct((tokens, width), half),
            jax.ShapeDtypeStruct((width, units), half),
            jax.ShapeDtypeStruct((units, width), half),
        ),
        in_specs=[VMEM] * 6,
        out_specs=(ANY,) * 4,
        scratch_shapes=[pltpu.VMEM((rows, width), half), DMA((4,))]
        + [DMA((2, 2, n_dp))] * 2
        + [DMA((2, n_tensor, 2 * n_dp - 1))] * 2
        + [DMA((2, n_dp))] * 2
        + [DMA((2, n_dp, n_groups))] * 2,
        compiler_params=pltpu.CompilerParams(collective_id=0, has_side_effects=True),
        name="gather_all",
    )(first_out, grad_second, w_up, w_down, gain, bias)

    preact = jnp.dot(normed, up, preferred_element_type=jnp.float32)
    hidden = jax.nn.gelu(preact).astype(half)
    grad_hidden = lax.dot_general(
        grad_all, down, (((1,), (1,)), ((), ())), preferred_element_type=jnp.float32
    )
    grad_pre = jax.vjp(jax.nn.gelu, preact)[1](grad_hidden)[0].astype(half)
    g_down = contract_tokens(hidden, grad_all).astype(half)
    g_up = contract_tokens(normed, grad_pre).astype(half)

    second_in, grad_first_in, grad_norm, up_out, down_out = pl.pallas_call(
        functools.partial(scatter_kernel, n_groups, n_tensor, n_dp, grad_scale),
        out_shape=(
            jax.ShapeDtypeStruct((rows, width), half),
            jax.ShapeDtypeStruct((rows, width), jnp.float32),
            jax.ShapeDtypeStruct((2, width), jnp.float32),
            jax.ShapeDtypeStruct((w_up.shape[0], w_up.shape[1]), half),
            jax.ShapeDtypeStruct((w_down.shape[0], w_down.shape[1]), half),
        ),
        in_specs=[VMEM] * 10,
        out_specs=(VMEM,) * 3 + (ANY,) * 2,
        scratch_shapes=[
            pltpu.VMEM((2, n_tensor, n_dp, rows, width), half),
            pltpu.VMEM((2, n_tensor - 1, n_dp, rows, width), half),
            pltpu.VMEM((2, n_dp - 1, rows, width), half),
            pltpu.VMEM((2, n_dp - 1, rows, width), half),
            pltpu.VMEM((n_dp, 8, width), jnp.float32),
            pltpu.VMEM((bits, 2, 8, width), jnp.float32),
            DMA((2,)),
        ]
        + [DMA((2, n_tensor - 1, n_dp))] * 2
        + [DMA((2, 2, n_dp - 1))] * 2
        + [DMA((2, n_dp))] * 2
        + [DMA((n_dp,))] * 2
        + [DMA((bits,))] * 2,
        compiler_params=pltpu.CompilerParams(collective_id=1, has_side_effects=True),
        name="scatter_all",
    )(hidden, grad_pre, up, down, g_up, g_down, first_out, second_out, grad_first, gain)
    grad_up = up_out.astype(jnp.float32) * grad_scale
    grad_down = down_out.astype(jnp.float32) * grad_scale
    return second_in, grad_first_in, grad_up, grad_down, grad_norm


def choose(sizes, *args):
    first_out, w_up = args[0], args[4]
    n_groups, n_tensor, n_dp = sizes
    tokens = first_out.shape[0] * n_tensor * n_dp
    fits = (
        n_tensor > 1
        and n_dp > 1
        and n_tensor & (n_tensor - 1) == 0
        and w_up.shape[1] % (n_dp * n_groups * 128) == 0
        and w_up.shape[0] % (n_groups * 128) == 0
    )
    if fits and tokens <= w_up.shape[1]:
        return spread_body(sizes, *args)
    return body(*args)


def solution(mesh):
    in_specs = (
        P(("groups", "tensor", "dp"), None),
        P(("groups", "tensor", "dp"), None),
        P(("groups", "tensor", "dp"), None),
        P(("groups", "tensor", "dp"), None),
        P("dp", "tensor"),
        P("tensor", "dp"),
        P(),
        P(),
    )
    out_specs = (
        P(("groups", "tensor", "dp"), None),
        P(("groups", "tensor", "dp"), None),
        P(("groups", "dp"), "tensor"),
        P(("groups", "tensor"), "dp"),
        P("groups", None),
    )
    sizes = tuple(mesh.shape[name] for name in ("groups", "tensor", "dp"))
    return jax.shard_map(functools.partial(choose, sizes), mesh=mesh, in_specs=in_specs, out_specs=out_specs, check_vma=False)
```

```python
import functools

import jax
import jax.numpy as jnp
import numpy as np
from jax import lax
from jax.experimental import pallas as pl
from jax.experimental.pallas import tpu as pltpu
from jax.sharding import PartitionSpec as P

epsilon = 1e-06


def normalize(row_data, norm_gain, norm_bias):
    values = row_data.astype(jnp.float32)
    row_mean = jnp.mean(values, axis=-1, keepdims=True)
    centred = values - row_mean
    inv_std = lax.rsqrt(jnp.mean(centred * centred, axis=-1, keepdims=True) + epsilon)
    standard = centred * inv_std
    normed = (standard * norm_gain + norm_bias).astype(jnp.bfloat16)
    return (standard, inv_std, normed)


def contract_tokens(left_rows, right_rows):
    return lax.dot_general(
        left_rows, right_rows, (((0,), (0,)), ((), ())), preferred_element_type=jnp.float32
    )


def body(first_out, second_out, grad_first, grad_second, w_up, w_down, norm_gain, norm_bias):
    own_rows = first_out.shape[0]
    up_full, down_full = (
        lax.all_gather(w_up, "dp", axis=0, tiled=True),
        lax.all_gather(w_down, "dp", axis=1, tiled=True),
    )
    first_all, grad_all = (
        lax.all_gather(first_out, "tensor", axis=0, tiled=True),
        lax.all_gather(grad_second, "tensor", axis=0, tiled=True),
    )
    standard_all, inv_std_all, normed = normalize(first_all, norm_gain, norm_bias)
    offset = lax.axis_index("tensor") * own_rows
    standard = lax.dynamic_slice_in_dim(standard_all, offset, own_rows, 0)
    inv_std = lax.dynamic_slice_in_dim(inv_std_all, offset, own_rows, 0)
    preact = jnp.dot(normed, up_full, preferred_element_type=jnp.float32)
    hidden = jax.nn.gelu(preact).astype(jnp.bfloat16)
    branch = lax.psum_scatter(
        jnp.dot(hidden, down_full, preferred_element_type=jnp.float32).astype(jnp.bfloat16),
        "tensor",
        scatter_dimension=0,
        tiled=True,
    ).astype(jnp.float32)
    second_in = (second_out.astype(jnp.float32) - branch).astype(jnp.bfloat16)
    tokens = own_rows * lax.axis_size("tensor") * lax.axis_size("dp")
    grad_scale = tokens ** (-0.5)
    grad_down_part = contract_tokens(hidden, grad_all)
    grad_down = (
        lax.psum_scatter(
            grad_down_part.astype(jnp.bfloat16), "dp", scatter_dimension=1, tiled=True
        ).astype(jnp.float32)
        * grad_scale
    )
    grad_hidden = lax.dot_general(
        grad_all, down_full, (((1,), (1,)), ((), ())), preferred_element_type=jnp.float32
    )
    grad_pre = jax.vjp(jax.nn.gelu, preact)[1](grad_hidden)[0].astype(jnp.bfloat16)
    grad_up_part = contract_tokens(normed, grad_pre)
    grad_up = (
        lax.psum_scatter(
            grad_up_part.astype(jnp.bfloat16), "dp", scatter_dimension=0, tiled=True
        ).astype(jnp.float32)
        * grad_scale
    )
    grad_normed = lax.psum_scatter(
        lax.dot_general(
            grad_pre, up_full, (((1,), (1,)), ((), ())), preferred_element_type=jnp.float32
        ).astype(jnp.bfloat16),
        "tensor",
        scatter_dimension=0,
        tiled=True,
    ).astype(jnp.float32)
    grad_std = grad_normed * norm_gain
    grad_rows = inv_std * (
        grad_std
        - jnp.mean(grad_std, axis=-1, keepdims=True)
        - standard * jnp.mean(grad_std * standard, axis=-1, keepdims=True)
    )
    grad_first_in = grad_first.astype(jnp.float32) + grad_rows
    local_stats = jnp.stack([jnp.sum(grad_normed * standard, axis=0), jnp.sum(grad_normed, axis=0)])
    grad_norm = lax.psum(local_stats, ("tensor", "dp")) * grad_scale
    return (second_in, grad_first_in, grad_up, grad_down, grad_norm)


def span(index, size):
    return pl.ds(pl.multiple_of(index * size, size), size)


def flipped(index, mask, bits):
    for bit in range(bits):
        if mask >> bit & 1:
            step = 1 << bit
            index = index + (1 - 2 * ((index // step) % 2)) * step
    return index


def greet(n_groups, n_dp, bits, group, tensor, dp):
    barrier = pltpu.get_barrier_semaphore()
    peers = [{"dp": (dp + s) % n_dp} for s in range(1, n_dp)]
    peers += [{"tensor": flipped(tensor, 1 << bit, bits)} for bit in range(bits)]
    peers += [{"groups": (group + s) % n_groups} for s in range(1, n_groups)]
    for peer in peers:
        pl.semaphore_signal(
            barrier, inc=1, device_id=peer, device_id_type=pl.DeviceIdType.MESH
        )
    pl.semaphore_wait(barrier, len(peers))


def remote(src, dst, sems, index, peer):
    return pltpu.make_async_remote_copy(
        src_ref=src,
        dst_ref=dst,
        send_sem=sems[0].at[index],
        recv_sem=sems[1].at[index],
        device_id=peer,
        device_id_type=pl.DeviceIdType.MESH,
    )


def gather_tokens(
    n_groups, n_tensor, n_dp, use,
    first_ref, grad_ref, w_up_ref, w_down_ref, gain_ref, bias_ref,
    normed_all, grad_all, up_ref, down_ref,
    own_normed, local_sem, line_send, line_recv, column_send, column_recv,
    weight_send, weight_recv, share_send, share_recv,
):
    group, tensor, dp = (lax.axis_index(name) for name in ("groups", "tensor", "dp"))
    bits = n_tensor.bit_length() - 1
    rows = first_ref.shape[0]
    depth = w_up_ref.shape[0]
    units = w_up_ref.shape[1] // n_dp
    outputs = (normed_all, grad_all)
    line_sems, column_sems = (line_send, line_recv), (column_send, column_recv)
    weight_sems, share_sems = (weight_send, weight_recv), (share_send, share_recv)

    def block(a, mask, source):
        return outputs[a].at[span(flipped(tensor, mask, bits) * n_dp + source, rows), :]

    def place(k):
        if k == 0:
            return dp, None
        if k < n_dp:
            return dp - k, dp >= k
        return dp + (k - n_dp + 1), dp + (k - n_dp + 1) <= n_dp - 1

    def guarded(conditions, action):
        conditions = [c for c in conditions if c is not None]
        if not conditions:
            action()
        else:
            pl.when(functools.reduce(jnp.logical_and, conditions))(action)

    def line_copy(a, side, distance):
        if side == 0:
            source, target = dp - (distance - 1), dp + 1
        else:
            source, target = dp + (distance - 1), dp - 1
        src = grad_ref if a == 1 and distance == 1 else block(a, 0, source)
        return remote(src, block(a, 0, source), line_sems, (a, side, distance), {"dp": target})

    def line_send_conditions(side, distance):
        if side == 0:
            return [dp >= distance - 1 if distance > 1 else None, dp <= n_dp - 2]
        return [dp <= n_dp - distance if distance > 1 else None, dp >= 1]

    def column_copy(a, mask, k, bit):
        source, _ = place(k)
        src = grad_ref if a == 1 and mask == 0 and k == 0 else block(a, mask, source)
        return remote(
            src, block(a, mask, source), column_sems, (a, mask | 1 << bit, k),
            {"tensor": flipped(tensor, 1 << bit, bits)},
        )

    def column_arrival(a, mask, k):
        source, _ = place(k)
        bit = (mask & -mask).bit_length() - 1
        here = block(a, mask, source)
        return remote(
            here, here, column_sems, (a, mask, k), {"tensor": flipped(tensor, 1 << bit, bits)}
        )

    def next_bits(mask):
        top = bits if mask == 0 else (mask & -mask).bit_length() - 1
        return list(reversed(range(top)))

    def pass_on(a, mask, k):
        for bit in next_bits(mask):
            column_copy(a, mask, k, bit).start()

    part = depth // n_groups
    piece = units // n_groups

    def weight_views(kind, source, owner):
        if kind == 0:
            return up_ref.at[span(source * n_groups + owner, part), :]
        return down_ref.at[span(owner, piece), span(source, depth)]

    def weight_copy(kind, s):
        target = (dp + s) % n_dp
        if kind == 0:
            src = w_up_ref.at[span(group, part), span(target, units)]
        else:
            src = w_down_ref.at[span(target * n_groups + group, piece), :]
        return remote(src, weight_views(kind, dp, group), weight_sems, (kind, s), {"dp": target})

    def weight_arrival(kind, s):
        here = weight_views(kind, (dp + n_dp - s) % n_dp, group)
        return remote(here, here, weight_sems, (kind, s), {"dp": (dp + s) % n_dp})

    def share_copy(kind, s, h):
        here = weight_views(kind, (dp + n_dp - s) % n_dp, group)
        return remote(here, here, share_sems, (kind, s, h), {"groups": (group + h) % n_groups})

    def share_arrival(kind, s, h):
        here = weight_views(kind, (dp + n_dp - s) % n_dp, (group + n_groups - h) % n_groups)
        return remote(here, here, share_sems, (kind, s, h), {"groups": (group + h) % n_groups})

    greet(n_groups, n_dp, bits, group, tensor, dp)
    order = [0] + [k for s in range(1, n_dp) for k in (s, s + n_dp - 1)]
    def send_own(a):
        for side in range(2):
            guarded(
                line_send_conditions(side, 1), lambda side=side: line_copy(a, side, 1).start()
            )
        pass_on(a, 0, 0)

    send_own(1)
    local = [
        pltpu.make_async_copy(grad_ref, block(1, 0, dp), local_sem.at[1]),
        pltpu.make_async_copy(
            w_up_ref.at[:, span(dp, units)], up_ref.at[span(dp, depth), :], local_sem.at[2]
        ),
        pltpu.make_async_copy(
            w_down_ref.at[span(dp, units), :], down_ref.at[:, span(dp, depth)], local_sem.at[3]
        ),
    ]
    for copy in local:
        copy.start()

    @pl.loop(0, rows // 16)
    def _(i):
        cut = pl.ds(pl.multiple_of(i * 16, 16), 16)
        standard, _ = standardize(first_ref[cut, :])
        own_normed[cut, :] = (standard * gain_ref[...] + bias_ref[...]).astype(own_normed.dtype)

    settle = pltpu.make_async_copy(own_normed, block(0, 0, dp), local_sem.at[0])
    settle.start()
    settle.wait()
    send_own(0)
    for s in range(1, n_dp):
        for kind in range(2):
            weight_copy(kind, s).start()

    through = [m for m in range(1, n_tensor) if next_bits(m)]
    final = [m for m in range(1, n_tensor) if not next_bits(m)]

    def relay(k):
        for a in range(2):
            for mask in sorted(through, reverse=True):
                def action(a=a, mask=mask):
                    column_arrival(a, mask, k).wait_recv()
                    pass_on(a, mask, k)
                guarded([place(k)[1]], action)

    done = [[0]] + [[s, s + n_dp - 1] for s in range(1, n_dp)]
    for s in range(1, n_dp):
        for a in range(2):
            for side in range(2):
                k = done[s][side]

                def action(a=a, side=side, k=k, s=s):
                    source, _ = place(k)
                    here = block(a, 0, source)
                    remote(here, here, line_sems, (a, side, s), {"dp": (dp + 1) % n_dp}).wait_recv()
                    if s < n_dp - 1:
                        guarded(
                            line_send_conditions(side, s + 1),
                            lambda: line_copy(a, side, s + 1).start(),
                        )
                    pass_on(a, 0, k)

                guarded([place(k)[1]], action)
        for k in done[s - 1]:
            relay(k)
        for kind in range(2):
            weight_arrival(kind, s).wait_recv()
            for h in range(1, n_groups):
                share_copy(kind, s, h).start()
    for k in done[n_dp - 1]:
        relay(k)
    for copy in local:
        copy.wait()
    for s in range(1, n_dp):
        for kind in range(2):
            for h in range(1, n_groups):
                share_arrival(kind, s, h).wait_recv()
    for mask in [0] + through:
        use(mask)
    for mask in final:
        for k in order:
            for a in range(2):
                guarded(
                    [place(k)[1]], lambda a=a, mask=mask, k=k: column_arrival(a, mask, k).wait_recv()
                )
        use(mask)
    for s in range(1, n_dp):
        for kind in range(2):
            weight_copy(kind, s).wait_send()
            for h in range(1, n_groups):
                share_copy(kind, s, h).wait_send()
    for a in range(2):
        for side in range(2):
            for s in range(1, n_dp):
                guarded(
                    line_send_conditions(side, s),
                    lambda a=a, side=side, s=s: line_copy(a, side, s).wait_send(),
                )
        for mask in [0] + through:
            for k in order:
                for bit in next_bits(mask):
                    guarded(
                        [place(k)[1]],
                        lambda a=a, mask=mask, k=k, bit=bit: column_copy(a, mask, k, bit).wait_send(),
                    )


def scatter_sums(
    n_groups, n_tensor, n_dp, grad_scale, weight_block,
    hidden_ref, pre_ref, up_ref, down_ref, g_up_ref, g_down_ref,
    first_ref, second_ref, grad_ref, gain_ref,
    second_in_ref, grad_first_ref, grad_norm_ref, up_out, down_out,
    partials, fold, right, left, stat_line, stat_fold, local_sem,
    fold_send, fold_recv, line_send, line_recv, grads_send, grads_recv,
    stat_send, stat_recv, pair_send, pair_recv,
):
    group, tensor, dp = (lax.axis_index(name) for name in ("groups", "tensor", "dp"))
    bits = n_tensor.bit_length() - 1
    rows, width = first_ref.shape
    units = g_up_ref.shape[2]
    depth = g_up_ref.shape[1]
    fold_sems, line_sems = (fold_send, fold_recv), (line_send, line_recv)
    grads_sems, stat_sems, pair_sems = (
        (grads_send, grads_recv), (stat_send, stat_recv), (pair_send, pair_recv),
    )
    slots = {}
    for bit in range(bits):
        for mask in range(0, n_tensor, 2 << bit):
            slots[bit, mask] = len(slots)

    def grads_copy(kind, s):
        target = (dp + s) % n_dp
        if kind == 0:
            src, dst = g_up_ref.at[target], up_out.at[:, span(dp, units)]
        else:
            src, dst = g_down_ref.at[target], down_out.at[span(dp, units), :]
        return remote(src, dst, grads_sems, (kind, s), {"dp": target})

    def grads_arrival(kind, s):
        source = (dp + n_dp - s) % n_dp
        here = up_out.at[:, span(source, units)] if kind == 0 else down_out.at[span(source, units), :]
        return remote(here, here, grads_sems, (kind, s), {"dp": (dp + s) % n_dp})

    def current(a, bit, mask, b):
        if bit == 0:
            return partials.at[a, mask, b]
        return fold.at[a, slots[bit - 1, mask], b]

    def fold_copy(a, bit, mask, b):
        slot = slots[bit, mask ^ 1 << bit]
        return remote(
            current(a, bit, mask, b), fold.at[a, slot, b], fold_sems, (a, slot, b),
            {"tensor": flipped(tensor, 1 << bit, bits)},
        )

    def fold_arrival(a, bit, mask, b):
        slot = slots[bit, mask]
        here = fold.at[a, slot, b]
        return remote(
            here, here, fold_sems, (a, slot, b), {"tensor": flipped(tensor, 1 << bit, bits)}
        )

    def add_into(ref, other):
        @pl.loop(0, rows // 16)
        def _(i):
            cut = pl.ds(pl.multiple_of(i * 16, 16), 16)
            ref[cut, :] = (
                ref[cut, :].astype(jnp.float32) + other[cut, :].astype(jnp.float32)
            ).astype(ref.dtype)

    def sent_masks(bit):
        masks = [m for m in range(n_tensor) if m % (1 << bit) == 0 and m >> bit & 1]
        return sorted(masks, reverse=True)

    def kept_masks(bit):
        return sorted(range(0, n_tensor, 2 << bit), reverse=True)

    @pl.loop(1, n_dp)
    def _(s):
        weight_block(0, (dp + s) % n_dp)
        grads_copy(0, s).start()

    @pl.loop(1, n_dp + 1)
    def _(s):
        weight_block(1, (dp + s) % n_dp)

    weight_block(0, dp)
    local = [
        pltpu.make_async_copy(g_up_ref.at[dp], up_out.at[:, span(dp, units)], local_sem.at[0]),
        pltpu.make_async_copy(g_down_ref.at[dp], down_out.at[span(dp, units), :], local_sem.at[1]),
    ]
    for copy in local:
        copy.start()

    way = 2 * ((2 * dp) // n_dp) - 1

    def multiply(mask, b):
        cut = span(flipped(tensor, mask, bits) * n_dp + b, rows)
        partials[0, mask, b] = jnp.dot(
            hidden_ref[cut, :], down_ref[...], preferred_element_type=jnp.float32
        ).astype(partials.dtype)
        partials[1, mask, b] = lax.dot_general(
            pre_ref[cut, :], up_ref[...], (((1,), (1,)), ((), ())),
            preferred_element_type=jnp.float32,
        ).astype(partials.dtype)

    def folded(bit, mask, b):
        for a in range(2):
            fold_arrival(a, bit, mask, b).wait_recv()
            add_into(fold.at[a, slots[bit, mask], b], current(a, bit, mask, b))
            if bit + 1 < bits and mask in sent_masks(bit + 1):
                fold_copy(a, bit + 1, mask, b).start()

    for mask in sent_masks(0):
        @pl.loop(0, n_dp)
        def _(i, mask=mask):
            b = (dp + way * (1 + i) + n_dp) % n_dp
            multiply(mask, b)
            for a in range(2):
                fold_copy(a, 0, mask, b).start()

        @pl.loop(0, n_dp)
        def _(i, mask=mask):
            b = (dp + way * (1 + i) + n_dp) % n_dp
            multiply(mask - 1, b)
            folded(0, mask - 1, b)

    for bit in range(1, bits - 1):
        for mask in kept_masks(bit):
            for i in range(n_dp):
                folded(bit, mask, (dp + way * (1 + i) + n_dp) % n_dp)

    def finish(b):
        if bits > 1:
            folded(bits - 1, 0, b)

    last = slots[bits - 1, 0]
    moving = (right, left)

    def line_conditions(side, s):
        return dp + s <= n_dp - 1 if side == 0 else dp >= s

    def behind(side):
        return dp >= 1 if side == 0 else dp <= n_dp - 2

    def line_peer(side):
        return {"dp": (dp + 1) % n_dp if side == 0 else (dp + n_dp - 1) % n_dp}

    def line_copy(a, side, s, relayed):
        target = dp + s if side == 0 else dp - s
        src = moving[side].at[a, s] if relayed else fold.at[a, last, target]
        return remote(src, moving[side].at[a, s - 1], line_sems, (a, side, s - 1), line_peer(side))

    def line_arrival(a, side, s):
        here = moving[side].at[a, s]
        return remote(here, here, line_sems, (a, side, s), line_peer(side))

    for s in range(n_dp - 1, 0, -1):
        for side in range(2):
            @pl.when(jnp.logical_and(line_conditions(side, s), jnp.logical_not(behind(side))))
            def _(side=side, s=s):
                finish(dp + s if side == 0 else dp - s)
                for a in range(2):
                    line_copy(a, side, s, False).start()

            if s <= n_dp - 2:
                @pl.when(jnp.logical_and(line_conditions(side, s), behind(side)))
                def _(side=side, s=s):
                    target = dp + s if side == 0 else dp - s
                    finish(target)
                    for a in range(2):
                        line_arrival(a, side, s).wait_recv()
                        add_into(moving[side].at[a, s], fold.at[a, last, target])
                        line_copy(a, side, s, True).start()
        grads_copy(1, s).start()
    finish(dp)

    for a in range(2):
        for side in range(2):
            @pl.when(behind(side))
            def _(a=a, side=side):
                line_arrival(a, side, 0).wait_recv()

            @pl.when(jnp.logical_not(behind(side)))
            def _(a=a, side=side):
                moving[side][a, 0] = jnp.zeros((rows, width), moving[side].dtype)

    stat_line[dp] = jnp.zeros(stat_line.shape[1:], jnp.float32)

    @pl.loop(0, rows // 16)
    def _(i):
        cut = pl.ds(pl.multiple_of(i * 16, 16), 16)

        def total(a):
            return (
                fold[a, last, dp, cut, :].astype(jnp.float32)
                + right[a, 0, cut, :].astype(jnp.float32)
                + left[a, 0, cut, :].astype(jnp.float32)
            )

        second_in_ref[cut, :] = (second_ref[cut, :].astype(jnp.float32) - total(0)).astype(
            second_in_ref.dtype
        )
        standard, inv_std = standardize(first_ref[cut, :])
        grad_normed = total(1)
        stat_line[dp, 0:1, :] += jnp.sum(grad_normed * standard, axis=0, keepdims=True)
        stat_line[dp, 1:2, :] += jnp.sum(grad_normed, axis=0, keepdims=True)
        grad_std = grad_normed * gain_ref[...]
        grad_rows = inv_std * (
            grad_std
            - jnp.mean(grad_std, axis=-1, keepdims=True)
            - standard * jnp.mean(grad_std * standard, axis=-1, keepdims=True)
        )
        grad_first_ref[cut, :] = grad_ref[cut, :].astype(jnp.float32) + grad_rows

    def stat_copy(s):
        here = stat_line.at[dp]
        return remote(here, here, stat_sems, s, {"dp": (dp + s) % n_dp})

    def stat_arrival(s):
        here = stat_line.at[(dp + n_dp - s) % n_dp]
        return remote(here, here, stat_sems, s, {"dp": (dp + s) % n_dp})

    for s in range(1, n_dp):
        stat_copy(s).start()
    for s in range(1, n_dp):
        stat_arrival(s).wait_recv()
    sums = stat_line[0]
    for source in range(1, n_dp):
        sums = sums + stat_line[source]
    for bit in range(bits):
        stat_fold[bit, 0] = sums
        copy = remote(
            stat_fold.at[bit, 0], stat_fold.at[bit, 1], pair_sems, bit,
            {"tensor": flipped(tensor, 1 << bit, bits)},
        )
        copy.start()
        copy.wait()
        sums = stat_fold[bit, 0] + stat_fold[bit, 1]
    grad_norm_ref[...] = sums[0:2] * grad_scale

    for s in range(1, n_dp):
        stat_copy(s).wait_send()
        for kind in range(2):
            grads_arrival(kind, s).wait_recv()
            grads_copy(kind, s).wait_send()
    for copy in local:
        copy.wait()
    for bit in range(bits):
        for mask in sent_masks(bit):
            for b in range(n_dp):
                for a in range(2):
                    fold_copy(a, bit, mask, b).wait_send()
    for s in range(n_dp - 1, 0, -1):
        for a in range(2):
            for side in range(2):
                @pl.when(line_conditions(side, s))
                def _(a=a, side=side, s=s):
                    line_copy(a, side, s, s <= n_dp - 2).wait_send()


def standardize(row_data):
    values = row_data.astype(jnp.float32)
    centred = values - jnp.mean(values, axis=-1, keepdims=True)
    inv_std = lax.rsqrt(jnp.mean(centred * centred, axis=-1, keepdims=True) + epsilon)
    return centred * inv_std, inv_std


def fused_kernel(
    n_groups, n_tensor, n_dp, grad_scale,
    first_ref, second_ref, grad_first_in_ref, grad_ref, w_up_ref, w_down_ref, gain_ref, bias_ref,
    second_in_ref, grad_first_ref, grad_norm_ref, up_out, down_out,
    normed_all, grad_all, up_ref, down_ref, hidden_ref, pre_ref, g_up_ref, g_down_ref,
    *scratch,
):
    tensor = lax.axis_index("tensor")
    bits = n_tensor.bit_length() - 1
    column = first_ref.shape[0] * n_dp
    chunk = column // 2
    depth = g_up_ref.shape[1]
    gather_count = 10

    def use(mask):
        base = flipped(tensor, mask, bits)

        @pl.loop(0, column // chunk)
        def _(i):
            cut = span(base * (column // chunk) + i, chunk)
            preact = jnp.dot(
                normed_all[cut, :], up_ref[...], preferred_element_type=jnp.float32
            )
            grad_hidden = lax.dot_general(
                grad_all[cut, :], down_ref[...], (((1,), (1,)), ((), ())),
                preferred_element_type=jnp.float32,
            )
            root = (2.0 / np.pi) ** 0.5
            square = preact * preact
            bend = jnp.tanh(root * (preact + 0.044715 * (square * preact)))
            gate = 0.5 * (1.0 + bend)
            hidden_ref[cut, :] = (preact * gate).astype(hidden_ref.dtype)
            slope = gate + (0.5 * preact) * (1.0 - bend * bend) * (
                root * (1.0 + 3.0 * 0.044715 * square)
            )
            pre_ref[cut, :] = (grad_hidden * slope).astype(pre_ref.dtype)

    def weight_block(kind, target):
        cut = span(target, depth)
        if kind == 0:
            g_up_ref[target] = contract_tokens(normed_all[:, cut], pre_ref[...]).astype(g_up_ref.dtype)
        else:
            g_down_ref[target] = contract_tokens(hidden_ref[...], grad_all[:, cut]).astype(
                g_down_ref.dtype
            )

    gather_tokens(
        n_groups, n_tensor, n_dp, use,
        first_ref, grad_ref, w_up_ref, w_down_ref, gain_ref, bias_ref,
        normed_all, grad_all, up_ref, down_ref, *scratch[:gather_count],
    )
    scatter_sums(
        n_groups, n_tensor, n_dp, grad_scale, weight_block,
        hidden_ref, pre_ref, up_ref, down_ref, g_up_ref, g_down_ref,
        first_ref, second_ref, grad_first_in_ref, gain_ref,
        second_in_ref, grad_first_ref, grad_norm_ref, up_out, down_out, *scratch[gather_count:],
    )


ANY = pl.BlockSpec(memory_space=pl.ANY)
VMEM = pl.BlockSpec(memory_space=pltpu.VMEM)
DMA = pltpu.SemaphoreType.DMA


def spread_body(sizes, first_out, second_out, grad_first, grad_second, w_up, w_down, norm_gain, norm_bias):
    n_groups, n_tensor, n_dp = sizes
    rows, width = first_out.shape
    tokens = rows * n_tensor * n_dp
    units = w_up.shape[1] // n_dp
    bits = n_tensor.bit_length() - 1
    half = jnp.bfloat16
    grad_scale = tokens ** (-0.5)
    gain, bias = norm_gain.reshape(1, -1), norm_bias.reshape(1, -1)
    depth = w_up.shape[0]
    second_in, grad_first_in, grad_norm, up_out, down_out = pl.pallas_call(
        functools.partial(fused_kernel, n_groups, n_tensor, n_dp, grad_scale),
        out_shape=(
            jax.ShapeDtypeStruct((rows, width), half),
            jax.ShapeDtypeStruct((rows, width), jnp.float32),
            jax.ShapeDtypeStruct((2, width), jnp.float32),
            jax.ShapeDtypeStruct(w_up.shape, half),
            jax.ShapeDtypeStruct(w_down.shape, half),
        ),
        in_specs=[VMEM] * 8,
        out_specs=(VMEM,) * 3 + (ANY,) * 2,
        scratch_shapes=[
            pltpu.VMEM((tokens, width), half),
            pltpu.VMEM((tokens, width), half),
            pltpu.VMEM((width, units), half),
            pltpu.VMEM((units, width), half),
            pltpu.VMEM((tokens, units), half),
            pltpu.VMEM((tokens, units), half),
            pltpu.VMEM((n_dp, depth, units), half),
            pltpu.VMEM((n_dp, units, depth), half),
        ]
        + [pltpu.VMEM((rows, width), half), DMA((4,))]
        + [DMA((2, 2, n_dp))] * 2
        + [DMA((2, n_tensor, 2 * n_dp - 1))] * 2
        + [DMA((2, n_dp))] * 2
        + [DMA((2, n_dp, n_groups))] * 2
        + [
            pltpu.VMEM((2, n_tensor, n_dp, rows, width), half),
            pltpu.VMEM((2, n_tensor - 1, n_dp, rows, width), half),
            pltpu.VMEM((2, n_dp - 1, rows, width), half),
            pltpu.VMEM((2, n_dp - 1, rows, width), half),
            pltpu.VMEM((n_dp, 8, width), jnp.float32),
            pltpu.VMEM((bits, 2, 8, width), jnp.float32),
            DMA((2,)),
        ]
        + [DMA((2, n_tensor - 1, n_dp))] * 2
        + [DMA((2, 2, n_dp - 1))] * 2
        + [DMA((2, n_dp))] * 2
        + [DMA((n_dp,))] * 2
        + [DMA((bits,))] * 2,
        compiler_params=pltpu.CompilerParams(
            collective_id=0, has_side_effects=True, vmem_limit_bytes=60 << 20
        ),
        name="spread_backward",
    )(first_out, second_out, grad_first, grad_second, w_up, w_down, gain, bias)
    grad_up = up_out.astype(jnp.float32) * grad_scale
    grad_down = down_out.astype(jnp.float32) * grad_scale
    return second_in, grad_first_in, grad_up, grad_down, grad_norm


def choose(sizes, *args):
    first_out, w_up = args[0], args[4]
    n_groups, n_tensor, n_dp = sizes
    tokens = first_out.shape[0] * n_tensor * n_dp
    fits = (
        n_tensor > 1
        and n_dp > 1
        and n_dp % 2 == 0
        and n_tensor & (n_tensor - 1) == 0
        and w_up.shape[1] % (n_dp * n_groups * 128) == 0
        and w_up.shape[0] % (n_groups * 128) == 0
    )
    if fits and tokens <= w_up.shape[1]:
        return spread_body(sizes, *args)
    return body(*args)


def solution(mesh):
    in_specs = (
        P(("groups", "tensor", "dp"), None),
        P(("groups", "tensor", "dp"), None),
        P(("groups", "tensor", "dp"), None),
        P(("groups", "tensor", "dp"), None),
        P("dp", "tensor"),
        P("tensor", "dp"),
        P(),
        P(),
    )
    out_specs = (
        P(("groups", "tensor", "dp"), None),
        P(("groups", "tensor", "dp"), None),
        P(("groups", "dp"), "tensor"),
        P(("groups", "tensor"), "dp"),
        P("groups", None),
    )
    sizes = tuple(mesh.shape[name] for name in ("groups", "tensor", "dp"))
    return jax.shard_map(functools.partial(choose, sizes), mesh=mesh, in_specs=in_specs, out_specs=out_specs, check_vma=False)
```

```python
import functools

import jax
import jax.numpy as jnp
import numpy as np
from jax import lax
from jax.experimental import pallas as pl
from jax.experimental.pallas import tpu as pltpu
from jax.sharding import PartitionSpec as P

epsilon = 1e-06


def normalize(row_data, norm_gain, norm_bias):
    values = row_data.astype(jnp.float32)
    row_mean = jnp.mean(values, axis=-1, keepdims=True)
    centred = values - row_mean
    inv_std = lax.rsqrt(jnp.mean(centred * centred, axis=-1, keepdims=True) + epsilon)
    standard = centred * inv_std
    normed = (standard * norm_gain + norm_bias).astype(jnp.bfloat16)
    return (standard, inv_std, normed)


def contract_tokens(left_rows, right_rows):
    return lax.dot_general(
        left_rows, right_rows, (((0,), (0,)), ((), ())), preferred_element_type=jnp.float32
    )


def body(first_out, second_out, grad_first, grad_second, w_up, w_down, norm_gain, norm_bias):
    own_rows = first_out.shape[0]
    up_full, down_full = (
        lax.all_gather(w_up, "dp", axis=0, tiled=True),
        lax.all_gather(w_down, "dp", axis=1, tiled=True),
    )
    first_all, grad_all = (
        lax.all_gather(first_out, "tensor", axis=0, tiled=True),
        lax.all_gather(grad_second, "tensor", axis=0, tiled=True),
    )
    standard_all, inv_std_all, normed = normalize(first_all, norm_gain, norm_bias)
    offset = lax.axis_index("tensor") * own_rows
    standard = lax.dynamic_slice_in_dim(standard_all, offset, own_rows, 0)
    inv_std = lax.dynamic_slice_in_dim(inv_std_all, offset, own_rows, 0)
    preact = jnp.dot(normed, up_full, preferred_element_type=jnp.float32)
    hidden = jax.nn.gelu(preact).astype(jnp.bfloat16)
    branch = lax.psum_scatter(
        jnp.dot(hidden, down_full, preferred_element_type=jnp.float32).astype(jnp.bfloat16),
        "tensor",
        scatter_dimension=0,
        tiled=True,
    ).astype(jnp.float32)
    second_in = (second_out.astype(jnp.float32) - branch).astype(jnp.bfloat16)
    tokens = own_rows * lax.axis_size("tensor") * lax.axis_size("dp")
    grad_scale = tokens ** (-0.5)
    grad_down_part = contract_tokens(hidden, grad_all)
    grad_down = (
        lax.psum_scatter(
            grad_down_part.astype(jnp.bfloat16), "dp", scatter_dimension=1, tiled=True
        ).astype(jnp.float32)
        * grad_scale
    )
    grad_hidden = lax.dot_general(
        grad_all, down_full, (((1,), (1,)), ((), ())), preferred_element_type=jnp.float32
    )
    grad_pre = jax.vjp(jax.nn.gelu, preact)[1](grad_hidden)[0].astype(jnp.bfloat16)
    grad_up_part = contract_tokens(normed, grad_pre)
    grad_up = (
        lax.psum_scatter(
            grad_up_part.astype(jnp.bfloat16), "dp", scatter_dimension=0, tiled=True
        ).astype(jnp.float32)
        * grad_scale
    )
    grad_normed = lax.psum_scatter(
        lax.dot_general(
            grad_pre, up_full, (((1,), (1,)), ((), ())), preferred_element_type=jnp.float32
        ).astype(jnp.bfloat16),
        "tensor",
        scatter_dimension=0,
        tiled=True,
    ).astype(jnp.float32)
    grad_std = grad_normed * norm_gain
    grad_rows = inv_std * (
        grad_std
        - jnp.mean(grad_std, axis=-1, keepdims=True)
        - standard * jnp.mean(grad_std * standard, axis=-1, keepdims=True)
    )
    grad_first_in = grad_first.astype(jnp.float32) + grad_rows
    local_stats = jnp.stack([jnp.sum(grad_normed * standard, axis=0), jnp.sum(grad_normed, axis=0)])
    grad_norm = lax.psum(local_stats, ("tensor", "dp")) * grad_scale
    return (second_in, grad_first_in, grad_up, grad_down, grad_norm)


def span(index, size):
    return pl.ds(pl.multiple_of(index * size, size), size)


def flipped(index, mask, bits):
    for bit in range(bits):
        if mask >> bit & 1:
            step = 1 << bit
            index = index + (1 - 2 * ((index // step) % 2)) * step
    return index


def greet(n_groups, n_dp, bits, group, tensor, dp):
    barrier = pltpu.get_barrier_semaphore()
    peers = [{"dp": (dp + s) % n_dp} for s in range(1, n_dp)]
    peers += [{"tensor": flipped(tensor, 1 << bit, bits)} for bit in range(bits)]
    peers += [{"groups": (group + s) % n_groups} for s in range(1, n_groups)]
    for peer in peers:
        pl.semaphore_signal(
            barrier, inc=1, device_id=peer, device_id_type=pl.DeviceIdType.MESH
        )
    pl.semaphore_wait(barrier, len(peers))


def remote(src, dst, sems, index, peer):
    return pltpu.make_async_remote_copy(
        src_ref=src,
        dst_ref=dst,
        send_sem=sems[0].at[index],
        recv_sem=sems[1].at[index],
        device_id=peer,
        device_id_type=pl.DeviceIdType.MESH,
    )


def gather_tokens(
    n_groups, n_tensor, n_dp, use,
    first_ref, grad_ref, w_up_ref, w_down_ref, gain_ref, bias_ref,
    normed_all, grad_all, up_ref, down_ref,
    own_normed, local_sem, line_send, line_recv, column_send, column_recv,
    weight_send, weight_recv, share_send, share_recv,
):
    group, tensor, dp = (lax.axis_index(name) for name in ("groups", "tensor", "dp"))
    bits = n_tensor.bit_length() - 1
    rows = first_ref.shape[0]
    depth = w_up_ref.shape[0]
    units = w_up_ref.shape[1] // n_dp
    outputs = (normed_all, grad_all)
    line_sems, column_sems = (line_send, line_recv), (column_send, column_recv)
    weight_sems, share_sems = (weight_send, weight_recv), (share_send, share_recv)

    def block(a, mask, source):
        return outputs[a].at[span(flipped(tensor, mask, bits) * n_dp + source, rows), :]

    def place(k):
        if k == 0:
            return dp, None
        if k < n_dp:
            return dp - k, dp >= k
        return dp + (k - n_dp + 1), dp + (k - n_dp + 1) <= n_dp - 1

    def guarded(conditions, action):
        conditions = [c for c in conditions if c is not None]
        if not conditions:
            action()
        else:
            pl.when(functools.reduce(jnp.logical_and, conditions))(action)

    def line_copy(a, side, distance):
        if side == 0:
            source, target = dp - (distance - 1), dp + 1
        else:
            source, target = dp + (distance - 1), dp - 1
        src = grad_ref if a == 1 and distance == 1 else block(a, 0, source)
        return remote(src, block(a, 0, source), line_sems, (a, side, distance), {"dp": target})

    def line_send_conditions(side, distance):
        if side == 0:
            return [dp >= distance - 1 if distance > 1 else None, dp <= n_dp - 2]
        return [dp <= n_dp - distance if distance > 1 else None, dp >= 1]

    def column_copy(a, mask, k, bit):
        source, _ = place(k)
        src = grad_ref if a == 1 and mask == 0 and k == 0 else block(a, mask, source)
        return remote(
            src, block(a, mask, source), column_sems, (a, mask | 1 << bit, k),
            {"tensor": flipped(tensor, 1 << bit, bits)},
        )

    def column_arrival(a, mask, k):
        source, _ = place(k)
        bit = (mask & -mask).bit_length() - 1
        here = block(a, mask, source)
        return remote(
            here, here, column_sems, (a, mask, k), {"tensor": flipped(tensor, 1 << bit, bits)}
        )

    def next_bits(mask):
        top = bits if mask == 0 else (mask & -mask).bit_length() - 1
        return list(reversed(range(top)))

    def pass_on(a, mask, k):
        for bit in next_bits(mask):
            column_copy(a, mask, k, bit).start()

    part = depth // n_groups
    piece = units // n_groups

    def weight_views(kind, source, owner):
        if kind == 0:
            return up_ref.at[span(source * n_groups + owner, part), :]
        return down_ref.at[span(owner, piece), span(source, depth)]

    def weight_copy(kind, s):
        target = (dp + s) % n_dp
        if kind == 0:
            src = w_up_ref.at[span(group, part), span(target, units)]
        else:
            src = w_down_ref.at[span(target * n_groups + group, piece), :]
        return remote(src, weight_views(kind, dp, group), weight_sems, (kind, s), {"dp": target})

    def weight_arrival(kind, s):
        here = weight_views(kind, (dp + n_dp - s) % n_dp, group)
        return remote(here, here, weight_sems, (kind, s), {"dp": (dp + s) % n_dp})

    def share_copy(kind, s, h):
        here = weight_views(kind, (dp + n_dp - s) % n_dp, group)
        return remote(here, here, share_sems, (kind, s, h), {"groups": (group + h) % n_groups})

    def share_arrival(kind, s, h):
        here = weight_views(kind, (dp + n_dp - s) % n_dp, (group + n_groups - h) % n_groups)
        return remote(here, here, share_sems, (kind, s, h), {"groups": (group + h) % n_groups})

    greet(n_groups, n_dp, bits, group, tensor, dp)
    order = [0] + [k for s in range(1, n_dp) for k in (s, s + n_dp - 1)]
    def send_own(a):
        for side in range(2):
            guarded(
                line_send_conditions(side, 1), lambda side=side: line_copy(a, side, 1).start()
            )
        pass_on(a, 0, 0)

    send_own(1)
    local = [
        pltpu.make_async_copy(grad_ref, block(1, 0, dp), local_sem.at[1]),
        pltpu.make_async_copy(
            w_up_ref.at[:, span(dp, units)], up_ref.at[span(dp, depth), :], local_sem.at[2]
        ),
        pltpu.make_async_copy(
            w_down_ref.at[span(dp, units), :], down_ref.at[:, span(dp, depth)], local_sem.at[3]
        ),
    ]
    for copy in local:
        copy.start()

    @pl.loop(0, rows // 16)
    def _(i):
        cut = pl.ds(pl.multiple_of(i * 16, 16), 16)
        standard, _ = standardize(first_ref[cut, :])
        own_normed[cut, :] = (standard * gain_ref[...] + bias_ref[...]).astype(own_normed.dtype)

    settle = pltpu.make_async_copy(own_normed, block(0, 0, dp), local_sem.at[0])
    settle.start()
    settle.wait()
    send_own(0)
    for s in range(1, n_dp):
        for kind in range(2):
            weight_copy(kind, s).start()

    through = [m for m in range(1, n_tensor) if next_bits(m)]
    final = [m for m in range(1, n_tensor) if not next_bits(m)]

    def relay(k):
        for a in range(2):
            for mask in sorted(through, reverse=True):
                def action(a=a, mask=mask):
                    column_arrival(a, mask, k).wait_recv()
                    pass_on(a, mask, k)
                guarded([place(k)[1]], action)

    done = [[0]] + [[s, s + n_dp - 1] for s in range(1, n_dp)]
    for s in range(1, n_dp):
        for a in range(2):
            for side in range(2):
                k = done[s][side]

                def action(a=a, side=side, k=k, s=s):
                    source, _ = place(k)
                    here = block(a, 0, source)
                    remote(here, here, line_sems, (a, side, s), {"dp": (dp + 1) % n_dp}).wait_recv()
                    if s < n_dp - 1:
                        guarded(
                            line_send_conditions(side, s + 1),
                            lambda: line_copy(a, side, s + 1).start(),
                        )
                    pass_on(a, 0, k)

                guarded([place(k)[1]], action)
        for k in done[s - 1]:
            relay(k)
        for kind in range(2):
            weight_arrival(kind, s).wait_recv()
            for h in range(1, n_groups):
                share_copy(kind, s, h).start()
    for k in done[n_dp - 1]:
        relay(k)
    for copy in local:
        copy.wait()
    for s in range(1, n_dp):
        for kind in range(2):
            for h in range(1, n_groups):
                share_arrival(kind, s, h).wait_recv()
    for mask in [0] + through:
        use(mask)
    for mask in final:
        for k in order:
            for a in range(2):
                guarded(
                    [place(k)[1]], lambda a=a, mask=mask, k=k: column_arrival(a, mask, k).wait_recv()
                )
        use(mask)
    for s in range(1, n_dp):
        for kind in range(2):
            weight_copy(kind, s).wait_send()
            for h in range(1, n_groups):
                share_copy(kind, s, h).wait_send()
    for a in range(2):
        for side in range(2):
            for s in range(1, n_dp):
                guarded(
                    line_send_conditions(side, s),
                    lambda a=a, side=side, s=s: line_copy(a, side, s).wait_send(),
                )
        for mask in [0] + through:
            for k in order:
                for bit in next_bits(mask):
                    guarded(
                        [place(k)[1]],
                        lambda a=a, mask=mask, k=k, bit=bit: column_copy(a, mask, k, bit).wait_send(),
                    )


def scatter_sums(
    n_groups, n_tensor, n_dp, grad_scale, weight_block,
    hidden_ref, pre_ref, up_ref, down_ref, g_up_ref, g_down_ref,
    first_ref, second_ref, grad_ref, gain_ref,
    second_in_ref, grad_first_ref, grad_norm_ref, up_out, down_out,
    partials, fold, right, left, stat_line, stat_fold, local_sem,
    fold_send, fold_recv, line_send, line_recv, grads_send, grads_recv,
    stat_send, stat_recv, pair_send, pair_recv,
):
    group, tensor, dp = (lax.axis_index(name) for name in ("groups", "tensor", "dp"))
    bits = n_tensor.bit_length() - 1
    rows, width = first_ref.shape
    units = g_up_ref.shape[2]
    depth = g_up_ref.shape[1]
    fold_sems, line_sems = (fold_send, fold_recv), (line_send, line_recv)
    grads_sems, stat_sems, pair_sems = (
        (grads_send, grads_recv), (stat_send, stat_recv), (pair_send, pair_recv),
    )
    slots = {}
    for bit in range(bits):
        for mask in range(0, n_tensor, 2 << bit):
            slots[bit, mask] = len(slots)

    def grads_copy(kind, s):
        target = (dp + s) % n_dp
        if kind == 0:
            src, dst = g_up_ref.at[target], up_out.at[:, span(dp, units)]
        else:
            src, dst = g_down_ref.at[target], down_out.at[span(dp, units), :]
        return remote(src, dst, grads_sems, (kind, s), {"dp": target})

    def grads_arrival(kind, s):
        source = (dp + n_dp - s) % n_dp
        here = up_out.at[:, span(source, units)] if kind == 0 else down_out.at[span(source, units), :]
        return remote(here, here, grads_sems, (kind, s), {"dp": (dp + s) % n_dp})

    def current(a, bit, mask, b):
        if bit == 0:
            return partials.at[a, mask, b]
        return fold.at[a, slots[bit - 1, mask], b]

    def fold_copy(a, bit, mask, b):
        slot = slots[bit, mask ^ 1 << bit]
        return remote(
            current(a, bit, mask, b), fold.at[a, slot, b], fold_sems, (a, slot, b),
            {"tensor": flipped(tensor, 1 << bit, bits)},
        )

    def fold_arrival(a, bit, mask, b):
        slot = slots[bit, mask]
        here = fold.at[a, slot, b]
        return remote(
            here, here, fold_sems, (a, slot, b), {"tensor": flipped(tensor, 1 << bit, bits)}
        )

    def add_into(ref, other):
        @pl.loop(0, rows // 16)
        def _(i):
            cut = pl.ds(pl.multiple_of(i * 16, 16), 16)
            ref[cut, :] = (
                ref[cut, :].astype(jnp.float32) + other[cut, :].astype(jnp.float32)
            ).astype(ref.dtype)

    def sent_masks(bit):
        masks = [m for m in range(n_tensor) if m % (1 << bit) == 0 and m >> bit & 1]
        return sorted(masks, reverse=True)

    def kept_masks(bit):
        return sorted(range(0, n_tensor, 2 << bit), reverse=True)

    @pl.loop(1, n_dp)
    def _(s):
        weight_block(0, (dp + s) % n_dp)
        grads_copy(0, s).start()

    way = 2 * ((2 * dp) // n_dp) - 1

    def multiply(mask, b):
        cut = span(flipped(tensor, mask, bits) * n_dp + b, rows)
        partials[0, mask, b] = jnp.dot(
            hidden_ref[cut, :], down_ref[...], preferred_element_type=jnp.float32
        ).astype(partials.dtype)
        partials[1, mask, b] = lax.dot_general(
            pre_ref[cut, :], up_ref[...], (((1,), (1,)), ((), ())),
            preferred_element_type=jnp.float32,
        ).astype(partials.dtype)

    def folded(bit, mask, b):
        for a in range(2):
            fold_arrival(a, bit, mask, b).wait_recv()
            add_into(fold.at[a, slots[bit, mask], b], current(a, bit, mask, b))
            if bit + 1 < bits and mask in sent_masks(bit + 1):
                fold_copy(a, bit + 1, mask, b).start()

    for mask in sent_masks(0):
        @pl.loop(0, n_dp)
        def _(i, mask=mask):
            b = (dp + way * (1 + i) + n_dp) % n_dp
            multiply(mask, b)
            for a in range(2):
                fold_copy(a, 0, mask, b).start()

        @pl.loop(0, n_dp)
        def _(i, mask=mask):
            b = (dp + way * (1 + i) + n_dp) % n_dp
            multiply(mask - 1, b)
            folded(0, mask - 1, b)

    for bit in range(1, bits - 1):
        for mask in kept_masks(bit):
            for i in range(n_dp):
                folded(bit, mask, (dp + way * (1 + i) + n_dp) % n_dp)

    def finish(b):
        if bits > 1:
            folded(bits - 1, 0, b)

    last = slots[bits - 1, 0]
    moving = (right, left)

    def line_conditions(side, s):
        return dp + s <= n_dp - 1 if side == 0 else dp >= s

    def behind(side):
        return dp >= 1 if side == 0 else dp <= n_dp - 2

    def line_peer(side):
        return {"dp": (dp + 1) % n_dp if side == 0 else (dp + n_dp - 1) % n_dp}

    def line_copy(a, side, s, relayed):
        target = dp + s if side == 0 else dp - s
        src = moving[side].at[a, s] if relayed else fold.at[a, last, target]
        return remote(src, moving[side].at[a, s - 1], line_sems, (a, side, s - 1), line_peer(side))

    def line_arrival(a, side, s):
        here = moving[side].at[a, s]
        return remote(here, here, line_sems, (a, side, s), line_peer(side))

    for s in range(n_dp - 1, 0, -1):
        weight_block(1, (dp + s) % n_dp)
        for side in range(2):
            @pl.when(jnp.logical_and(line_conditions(side, s), jnp.logical_not(behind(side))))
            def _(side=side, s=s):
                finish(dp + s if side == 0 else dp - s)
                for a in range(2):
                    line_copy(a, side, s, False).start()

            if s <= n_dp - 2:
                @pl.when(jnp.logical_and(line_conditions(side, s), behind(side)))
                def _(side=side, s=s):
                    target = dp + s if side == 0 else dp - s
                    finish(target)
                    for a in range(2):
                        line_arrival(a, side, s).wait_recv()
                        add_into(moving[side].at[a, s], fold.at[a, last, target])
                        line_copy(a, side, s, True).start()
        grads_copy(1, s).start()
    weight_block(0, dp)
    weight_block(1, dp)
    local = [
        pltpu.make_async_copy(g_up_ref.at[dp], up_out.at[:, span(dp, units)], local_sem.at[0]),
        pltpu.make_async_copy(g_down_ref.at[dp], down_out.at[span(dp, units), :], local_sem.at[1]),
    ]
    for copy in local:
        copy.start()
    finish(dp)

    for a in range(2):
        for side in range(2):
            @pl.when(behind(side))
            def _(a=a, side=side):
                line_arrival(a, side, 0).wait_recv()

            @pl.when(jnp.logical_not(behind(side)))
            def _(a=a, side=side):
                moving[side][a, 0] = jnp.zeros((rows, width), moving[side].dtype)

    stat_line[dp] = jnp.zeros(stat_line.shape[1:], jnp.float32)

    @pl.loop(0, rows // 16)
    def _(i):
        cut = pl.ds(pl.multiple_of(i * 16, 16), 16)

        def total(a):
            return (
                fold[a, last, dp, cut, :].astype(jnp.float32)
                + right[a, 0, cut, :].astype(jnp.float32)
                + left[a, 0, cut, :].astype(jnp.float32)
            )

        second_in_ref[cut, :] = (second_ref[cut, :].astype(jnp.float32) - total(0)).astype(
            second_in_ref.dtype
        )
        standard, inv_std = standardize(first_ref[cut, :])
        grad_normed = total(1)
        stat_line[dp, 0:1, :] += jnp.sum(grad_normed * standard, axis=0, keepdims=True)
        stat_line[dp, 1:2, :] += jnp.sum(grad_normed, axis=0, keepdims=True)
        grad_std = grad_normed * gain_ref[...]
        grad_rows = inv_std * (
            grad_std
            - jnp.mean(grad_std, axis=-1, keepdims=True)
            - standard * jnp.mean(grad_std * standard, axis=-1, keepdims=True)
        )
        grad_first_ref[cut, :] = grad_ref[cut, :].astype(jnp.float32) + grad_rows

    def stat_copy(s):
        here = stat_line.at[dp]
        return remote(here, here, stat_sems, s, {"dp": (dp + s) % n_dp})

    def stat_arrival(s):
        here = stat_line.at[(dp + n_dp - s) % n_dp]
        return remote(here, here, stat_sems, s, {"dp": (dp + s) % n_dp})

    for s in range(1, n_dp):
        stat_copy(s).start()
    for s in range(1, n_dp):
        stat_arrival(s).wait_recv()
    sums = stat_line[0]
    for source in range(1, n_dp):
        sums = sums + stat_line[source]
    for bit in range(bits):
        stat_fold[bit, 0] = sums
        copy = remote(
            stat_fold.at[bit, 0], stat_fold.at[bit, 1], pair_sems, bit,
            {"tensor": flipped(tensor, 1 << bit, bits)},
        )
        copy.start()
        copy.wait()
        sums = stat_fold[bit, 0] + stat_fold[bit, 1]
    grad_norm_ref[...] = sums[0:2] * grad_scale

    for s in range(1, n_dp):
        stat_copy(s).wait_send()
        for kind in range(2):
            grads_arrival(kind, s).wait_recv()
            grads_copy(kind, s).wait_send()
    for copy in local:
        copy.wait()
    for bit in range(bits):
        for mask in sent_masks(bit):
            for b in range(n_dp):
                for a in range(2):
                    fold_copy(a, bit, mask, b).wait_send()
    for s in range(n_dp - 1, 0, -1):
        for a in range(2):
            for side in range(2):
                @pl.when(line_conditions(side, s))
                def _(a=a, side=side, s=s):
                    line_copy(a, side, s, s <= n_dp - 2).wait_send()


def standardize(row_data):
    values = row_data.astype(jnp.float32)
    centred = values - jnp.mean(values, axis=-1, keepdims=True)
    inv_std = lax.rsqrt(jnp.mean(centred * centred, axis=-1, keepdims=True) + epsilon)
    return centred * inv_std, inv_std


def fused_kernel(
    n_groups, n_tensor, n_dp, grad_scale,
    first_ref, second_ref, grad_first_in_ref, grad_ref, w_up_ref, w_down_ref, gain_ref, bias_ref,
    second_in_ref, grad_first_ref, grad_norm_ref, up_out, down_out,
    normed_all, grad_all, up_ref, down_ref, hidden_ref, pre_ref, g_up_ref, g_down_ref,
    *scratch,
):
    tensor = lax.axis_index("tensor")
    bits = n_tensor.bit_length() - 1
    column = first_ref.shape[0] * n_dp
    chunk = column // 2
    depth = g_up_ref.shape[1]
    gather_count = 10

    def use(mask):
        base = flipped(tensor, mask, bits)

        @pl.loop(0, column // chunk)
        def _(i):
            cut = span(base * (column // chunk) + i, chunk)
            preact = jnp.dot(
                normed_all[cut, :], up_ref[...], preferred_element_type=jnp.float32
            )
            grad_hidden = lax.dot_general(
                grad_all[cut, :], down_ref[...], (((1,), (1,)), ((), ())),
                preferred_element_type=jnp.float32,
            )
            root = (2.0 / np.pi) ** 0.5
            square = preact * preact
            bend = jnp.tanh(root * (preact + 0.044715 * (square * preact)))
            gate = 0.5 * (1.0 + bend)
            hidden_ref[cut, :] = (preact * gate).astype(hidden_ref.dtype)
            slope = gate + (0.5 * preact) * (1.0 - bend * bend) * (
                root * (1.0 + 3.0 * 0.044715 * square)
            )
            pre_ref[cut, :] = (grad_hidden * slope).astype(pre_ref.dtype)

    def weight_block(kind, target):
        cut = span(target, depth)
        if kind == 0:
            g_up_ref[target] = contract_tokens(normed_all[:, cut], pre_ref[...]).astype(g_up_ref.dtype)
        else:
            g_down_ref[target] = contract_tokens(hidden_ref[...], grad_all[:, cut]).astype(
                g_down_ref.dtype
            )

    gather_tokens(
        n_groups, n_tensor, n_dp, use,
        first_ref, grad_ref, w_up_ref, w_down_ref, gain_ref, bias_ref,
        normed_all, grad_all, up_ref, down_ref, *scratch[:gather_count],
    )
    scatter_sums(
        n_groups, n_tensor, n_dp, grad_scale, weight_block,
        hidden_ref, pre_ref, up_ref, down_ref, g_up_ref, g_down_ref,
        first_ref, second_ref, grad_first_in_ref, gain_ref,
        second_in_ref, grad_first_ref, grad_norm_ref, up_out, down_out, *scratch[gather_count:],
    )


ANY = pl.BlockSpec(memory_space=pl.ANY)
VMEM = pl.BlockSpec(memory_space=pltpu.VMEM)
DMA = pltpu.SemaphoreType.DMA


def spread_body(sizes, first_out, second_out, grad_first, grad_second, w_up, w_down, norm_gain, norm_bias):
    n_groups, n_tensor, n_dp = sizes
    rows, width = first_out.shape
    tokens = rows * n_tensor * n_dp
    units = w_up.shape[1] // n_dp
    bits = n_tensor.bit_length() - 1
    half = jnp.bfloat16
    grad_scale = tokens ** (-0.5)
    gain, bias = norm_gain.reshape(1, -1), norm_bias.reshape(1, -1)
    depth = w_up.shape[0]
    second_in, grad_first_in, grad_norm, up_out, down_out = pl.pallas_call(
        functools.partial(fused_kernel, n_groups, n_tensor, n_dp, grad_scale),
        out_shape=(
            jax.ShapeDtypeStruct((rows, width), half),
            jax.ShapeDtypeStruct((rows, width), jnp.float32),
            jax.ShapeDtypeStruct((2, width), jnp.float32),
            jax.ShapeDtypeStruct(w_up.shape, half),
            jax.ShapeDtypeStruct(w_down.shape, half),
        ),
        in_specs=[VMEM] * 8,
        out_specs=(VMEM,) * 3 + (ANY,) * 2,
        scratch_shapes=[
            pltpu.VMEM((tokens, width), half),
            pltpu.VMEM((tokens, width), half),
            pltpu.VMEM((width, units), half),
            pltpu.VMEM((units, width), half),
            pltpu.VMEM((tokens, units), half),
            pltpu.VMEM((tokens, units), half),
            pltpu.VMEM((n_dp, depth, units), half),
            pltpu.VMEM((n_dp, units, depth), half),
        ]
        + [pltpu.VMEM((rows, width), half), DMA((4,))]
        + [DMA((2, 2, n_dp))] * 2
        + [DMA((2, n_tensor, 2 * n_dp - 1))] * 2
        + [DMA((2, n_dp))] * 2
        + [DMA((2, n_dp, n_groups))] * 2
        + [
            pltpu.VMEM((2, n_tensor, n_dp, rows, width), half),
            pltpu.VMEM((2, n_tensor - 1, n_dp, rows, width), half),
            pltpu.VMEM((2, n_dp - 1, rows, width), half),
            pltpu.VMEM((2, n_dp - 1, rows, width), half),
            pltpu.VMEM((n_dp, 8, width), jnp.float32),
            pltpu.VMEM((bits, 2, 8, width), jnp.float32),
            DMA((2,)),
        ]
        + [DMA((2, n_tensor - 1, n_dp))] * 2
        + [DMA((2, 2, n_dp - 1))] * 2
        + [DMA((2, n_dp))] * 2
        + [DMA((n_dp,))] * 2
        + [DMA((bits,))] * 2,
        compiler_params=pltpu.CompilerParams(
            collective_id=0, has_side_effects=True, vmem_limit_bytes=60 << 20
        ),
        name="spread_backward",
    )(first_out, second_out, grad_first, grad_second, w_up, w_down, gain, bias)
    grad_up = up_out.astype(jnp.float32) * grad_scale
    grad_down = down_out.astype(jnp.float32) * grad_scale
    return second_in, grad_first_in, grad_up, grad_down, grad_norm


def choose(sizes, *args):
    first_out, w_up = args[0], args[4]
    n_groups, n_tensor, n_dp = sizes
    tokens = first_out.shape[0] * n_tensor * n_dp
    fits = (
        n_tensor > 1
        and n_dp > 1
        and n_dp % 2 == 0
        and n_tensor & (n_tensor - 1) == 0
        and w_up.shape[1] % (n_dp * n_groups * 128) == 0
        and w_up.shape[0] % (n_groups * 128) == 0
    )
    if fits and tokens <= w_up.shape[1]:
        return spread_body(sizes, *args)
    return body(*args)


def solution(mesh):
    in_specs = (
        P(("groups", "tensor", "dp"), None),
        P(("groups", "tensor", "dp"), None),
        P(("groups", "tensor", "dp"), None),
        P(("groups", "tensor", "dp"), None),
        P("dp", "tensor"),
        P("tensor", "dp"),
        P(),
        P(),
    )
    out_specs = (
        P(("groups", "tensor", "dp"), None),
        P(("groups", "tensor", "dp"), None),
        P(("groups", "dp"), "tensor"),
        P(("groups", "tensor"), "dp"),
        P("groups", None),
    )
    sizes = tuple(mesh.shape[name] for name in ("groups", "tensor", "dp"))
    return jax.shard_map(functools.partial(choose, sizes), mesh=mesh, in_specs=in_specs, out_specs=out_specs, check_vma=False)
```

```python
import functools

import jax
import jax.numpy as jnp
import numpy as np
from jax import lax
from jax.experimental import pallas as pl
from jax.experimental.pallas import tpu as pltpu
from jax.sharding import PartitionSpec as P

epsilon = 1e-06


def normalize(row_data, norm_gain, norm_bias):
    values = row_data.astype(jnp.float32)
    row_mean = jnp.mean(values, axis=-1, keepdims=True)
    centred = values - row_mean
    inv_std = lax.rsqrt(jnp.mean(centred * centred, axis=-1, keepdims=True) + epsilon)
    standard = centred * inv_std
    normed = (standard * norm_gain + norm_bias).astype(jnp.bfloat16)
    return (standard, inv_std, normed)


def contract_tokens(left_rows, right_rows):
    return lax.dot_general(
        left_rows, right_rows, (((0,), (0,)), ((), ())), preferred_element_type=jnp.float32
    )


def body(first_out, second_out, grad_first, grad_second, w_up, w_down, norm_gain, norm_bias):
    own_rows = first_out.shape[0]
    up_full, down_full = (
        lax.all_gather(w_up, "dp", axis=0, tiled=True),
        lax.all_gather(w_down, "dp", axis=1, tiled=True),
    )
    first_all, grad_all = (
        lax.all_gather(first_out, "tensor", axis=0, tiled=True),
        lax.all_gather(grad_second, "tensor", axis=0, tiled=True),
    )
    standard_all, inv_std_all, normed = normalize(first_all, norm_gain, norm_bias)
    offset = lax.axis_index("tensor") * own_rows
    standard = lax.dynamic_slice_in_dim(standard_all, offset, own_rows, 0)
    inv_std = lax.dynamic_slice_in_dim(inv_std_all, offset, own_rows, 0)
    preact = jnp.dot(normed, up_full, preferred_element_type=jnp.float32)
    hidden = jax.nn.gelu(preact).astype(jnp.bfloat16)
    branch = lax.psum_scatter(
        jnp.dot(hidden, down_full, preferred_element_type=jnp.float32).astype(jnp.bfloat16),
        "tensor",
        scatter_dimension=0,
        tiled=True,
    ).astype(jnp.float32)
    second_in = (second_out.astype(jnp.float32) - branch).astype(jnp.bfloat16)
    tokens = own_rows * lax.axis_size("tensor") * lax.axis_size("dp")
    grad_scale = tokens ** (-0.5)
    grad_down_part = contract_tokens(hidden, grad_all)
    grad_down = (
        lax.psum_scatter(
            grad_down_part.astype(jnp.bfloat16), "dp", scatter_dimension=1, tiled=True
        ).astype(jnp.float32)
        * grad_scale
    )
    grad_hidden = lax.dot_general(
        grad_all, down_full, (((1,), (1,)), ((), ())), preferred_element_type=jnp.float32
    )
    grad_pre = jax.vjp(jax.nn.gelu, preact)[1](grad_hidden)[0].astype(jnp.bfloat16)
    grad_up_part = contract_tokens(normed, grad_pre)
    grad_up = (
        lax.psum_scatter(
            grad_up_part.astype(jnp.bfloat16), "dp", scatter_dimension=0, tiled=True
        ).astype(jnp.float32)
        * grad_scale
    )
    grad_normed = lax.psum_scatter(
        lax.dot_general(
            grad_pre, up_full, (((1,), (1,)), ((), ())), preferred_element_type=jnp.float32
        ).astype(jnp.bfloat16),
        "tensor",
        scatter_dimension=0,
        tiled=True,
    ).astype(jnp.float32)
    grad_std = grad_normed * norm_gain
    grad_rows = inv_std * (
        grad_std
        - jnp.mean(grad_std, axis=-1, keepdims=True)
        - standard * jnp.mean(grad_std * standard, axis=-1, keepdims=True)
    )
    grad_first_in = grad_first.astype(jnp.float32) + grad_rows
    local_stats = jnp.stack([jnp.sum(grad_normed * standard, axis=0), jnp.sum(grad_normed, axis=0)])
    grad_norm = lax.psum(local_stats, ("tensor", "dp")) * grad_scale
    return (second_in, grad_first_in, grad_up, grad_down, grad_norm)


def span(index, size):
    return pl.ds(pl.multiple_of(index * size, size), size)


def flipped(index, mask, bits):
    for bit in range(bits):
        if mask >> bit & 1:
            step = 1 << bit
            index = index + (1 - 2 * ((index // step) % 2)) * step
    return index


def greet(n_groups, n_dp, bits, group, tensor, dp):
    barrier = pltpu.get_barrier_semaphore()
    peers = [{"dp": (dp + s) % n_dp} for s in range(1, n_dp)]
    peers += [{"tensor": flipped(tensor, 1 << bit, bits)} for bit in range(bits)]
    peers += [{"groups": (group + s) % n_groups} for s in range(1, n_groups)]
    for peer in peers:
        pl.semaphore_signal(
            barrier, inc=1, device_id=peer, device_id_type=pl.DeviceIdType.MESH
        )
    pl.semaphore_wait(barrier, len(peers))


def remote(src, dst, sems, index, peer):
    return pltpu.make_async_remote_copy(
        src_ref=src,
        dst_ref=dst,
        send_sem=sems[0].at[index],
        recv_sem=sems[1].at[index],
        device_id=peer,
        device_id_type=pl.DeviceIdType.MESH,
    )


def gather_tokens(
    n_groups, n_tensor, n_dp, use,
    first_ref, grad_ref, w_up_ref, w_down_ref, gain_ref, bias_ref,
    normed_all, grad_all, up_ref, down_ref,
    own_normed, local_sem, line_send, line_recv, column_send, column_recv,
    weight_send, weight_recv, share_send, share_recv,
):
    group, tensor, dp = (lax.axis_index(name) for name in ("groups", "tensor", "dp"))
    bits = n_tensor.bit_length() - 1
    rows = first_ref.shape[0]
    depth = w_up_ref.shape[0]
    units = w_up_ref.shape[1] // n_dp
    outputs = (normed_all, grad_all)
    line_sems, column_sems = (line_send, line_recv), (column_send, column_recv)
    weight_sems, share_sems = (weight_send, weight_recv), (share_send, share_recv)

    def block(a, mask, source):
        return outputs[a].at[span(flipped(tensor, mask, bits) * n_dp + source, rows), :]

    def place(k):
        if k == 0:
            return dp, None
        if k < n_dp:
            return dp - k, dp >= k
        return dp + (k - n_dp + 1), dp + (k - n_dp + 1) <= n_dp - 1

    def guarded(conditions, action):
        conditions = [c for c in conditions if c is not None]
        if not conditions:
            action()
        else:
            pl.when(functools.reduce(jnp.logical_and, conditions))(action)

    def line_copy(a, side, distance):
        if side == 0:
            source, target = dp - (distance - 1), dp + 1
        else:
            source, target = dp + (distance - 1), dp - 1
        src = grad_ref if a == 1 and distance == 1 else block(a, 0, source)
        return remote(src, block(a, 0, source), line_sems, (a, side, distance), {"dp": target})

    def line_send_conditions(side, distance):
        if side == 0:
            return [dp >= distance - 1 if distance > 1 else None, dp <= n_dp - 2]
        return [dp <= n_dp - distance if distance > 1 else None, dp >= 1]

    def column_copy(a, mask, k, bit):
        source, _ = place(k)
        src = grad_ref if a == 1 and mask == 0 and k == 0 else block(a, mask, source)
        return remote(
            src, block(a, mask, source), column_sems, (a, mask | 1 << bit, k),
            {"tensor": flipped(tensor, 1 << bit, bits)},
        )

    def column_arrival(a, mask, k):
        source, _ = place(k)
        bit = (mask & -mask).bit_length() - 1
        here = block(a, mask, source)
        return remote(
            here, here, column_sems, (a, mask, k), {"tensor": flipped(tensor, 1 << bit, bits)}
        )

    def next_bits(mask):
        top = bits if mask == 0 else (mask & -mask).bit_length() - 1
        return list(reversed(range(top)))

    def pass_on(a, mask, k):
        for bit in next_bits(mask):
            column_copy(a, mask, k, bit).start()

    part = depth // n_groups
    piece = units // n_groups

    def weight_views(kind, source, owner):
        if kind == 0:
            return up_ref.at[span(source * n_groups + owner, part), :]
        return down_ref.at[span(owner, piece), span(source, depth)]

    def weight_copy(kind, s):
        target = (dp + s) % n_dp
        if kind == 0:
            src = w_up_ref.at[span(group, part), span(target, units)]
        else:
            src = w_down_ref.at[span(target * n_groups + group, piece), :]
        return remote(src, weight_views(kind, dp, group), weight_sems, (kind, s), {"dp": target})

    def weight_arrival(kind, s):
        here = weight_views(kind, (dp + n_dp - s) % n_dp, group)
        return remote(here, here, weight_sems, (kind, s), {"dp": (dp + s) % n_dp})

    def share_copy(kind, s, h):
        here = weight_views(kind, (dp + n_dp - s) % n_dp, group)
        return remote(here, here, share_sems, (kind, s, h), {"groups": (group + h) % n_groups})

    def share_arrival(kind, s, h):
        here = weight_views(kind, (dp + n_dp - s) % n_dp, (group + n_groups - h) % n_groups)
        return remote(here, here, share_sems, (kind, s, h), {"groups": (group + h) % n_groups})

    greet(n_groups, n_dp, bits, group, tensor, dp)
    order = [0] + [k for s in range(1, n_dp) for k in (s, s + n_dp - 1)]
    def send_own(a):
        for side in range(2):
            guarded(
                line_send_conditions(side, 1), lambda side=side: line_copy(a, side, 1).start()
            )
        pass_on(a, 0, 0)

    send_own(1)
    local = [
        pltpu.make_async_copy(grad_ref, block(1, 0, dp), local_sem.at[1]),
        pltpu.make_async_copy(
            w_up_ref.at[:, span(dp, units)], up_ref.at[span(dp, depth), :], local_sem.at[2]
        ),
        pltpu.make_async_copy(
            w_down_ref.at[span(dp, units), :], down_ref.at[:, span(dp, depth)], local_sem.at[3]
        ),
    ]
    for copy in local:
        copy.start()

    @pl.loop(0, rows // 16)
    def _(i):
        cut = pl.ds(pl.multiple_of(i * 16, 16), 16)
        standard, _ = standardize(first_ref[cut, :])
        own_normed[cut, :] = (standard * gain_ref[...] + bias_ref[...]).astype(own_normed.dtype)

    settle = pltpu.make_async_copy(own_normed, block(0, 0, dp), local_sem.at[0])
    settle.start()
    settle.wait()
    send_own(0)

    def send_weights(s):
        for kind in range(2):
            weight_copy(kind, s).start()

    def share_weights(s):
        for kind in range(2):
            weight_arrival(kind, s).wait_recv()
            for h in range(1, n_groups):
                share_copy(kind, s, h).start()

    send_weights(1)

    through = [m for m in range(1, n_tensor) if next_bits(m)]
    final = [m for m in range(1, n_tensor) if not next_bits(m)]

    def relay(k):
        for a in range(2):
            for mask in sorted(through, reverse=True):
                def action(a=a, mask=mask):
                    column_arrival(a, mask, k).wait_recv()
                    pass_on(a, mask, k)
                guarded([place(k)[1]], action)

    done = [[0]] + [[s, s + n_dp - 1] for s in range(1, n_dp)]
    for s in range(1, n_dp):
        for a in range(2):
            for side in range(2):
                k = done[s][side]

                def action(a=a, side=side, k=k, s=s):
                    source, _ = place(k)
                    here = block(a, 0, source)
                    remote(here, here, line_sems, (a, side, s), {"dp": (dp + 1) % n_dp}).wait_recv()
                    if s < n_dp - 1:
                        guarded(
                            line_send_conditions(side, s + 1),
                            lambda: line_copy(a, side, s + 1).start(),
                        )
                    pass_on(a, 0, k)

                guarded([place(k)[1]], action)
        if s < n_dp - 1:
            send_weights(s + 1)
        for k in done[s - 1]:
            relay(k)
        if s > 1:
            share_weights(s - 1)
    share_weights(n_dp - 1)
    for k in done[n_dp - 1]:
        relay(k)
    for copy in local:
        copy.wait()
    for s in range(1, n_dp):
        for kind in range(2):
            for h in range(1, n_groups):
                share_arrival(kind, s, h).wait_recv()
    for mask in [0] + through:
        use(mask)
    for mask in final:
        for k in order:
            for a in range(2):
                guarded(
                    [place(k)[1]], lambda a=a, mask=mask, k=k: column_arrival(a, mask, k).wait_recv()
                )
        use(mask)
    for s in range(1, n_dp):
        for kind in range(2):
            weight_copy(kind, s).wait_send()
            for h in range(1, n_groups):
                share_copy(kind, s, h).wait_send()
    for a in range(2):
        for side in range(2):
            for s in range(1, n_dp):
                guarded(
                    line_send_conditions(side, s),
                    lambda a=a, side=side, s=s: line_copy(a, side, s).wait_send(),
                )
        for mask in [0] + through:
            for k in order:
                for bit in next_bits(mask):
                    guarded(
                        [place(k)[1]],
                        lambda a=a, mask=mask, k=k, bit=bit: column_copy(a, mask, k, bit).wait_send(),
                    )


def scatter_sums(
    n_groups, n_tensor, n_dp, grad_scale, weight_block,
    hidden_ref, pre_ref, up_ref, down_ref, g_up_ref, g_down_ref,
    first_ref, second_ref, grad_ref, gain_ref,
    second_in_ref, grad_first_ref, grad_norm_ref, up_out, down_out,
    partials, fold, right, left, stat_line, stat_fold, local_sem,
    fold_send, fold_recv, line_send, line_recv, grads_send, grads_recv,
    stat_send, stat_recv, pair_send, pair_recv,
):
    group, tensor, dp = (lax.axis_index(name) for name in ("groups", "tensor", "dp"))
    bits = n_tensor.bit_length() - 1
    rows, width = first_ref.shape
    units = g_up_ref.shape[2]
    depth = g_up_ref.shape[1]
    fold_sems, line_sems = (fold_send, fold_recv), (line_send, line_recv)
    grads_sems, stat_sems, pair_sems = (
        (grads_send, grads_recv), (stat_send, stat_recv), (pair_send, pair_recv),
    )
    slots = {}
    for bit in range(bits):
        for mask in range(0, n_tensor, 2 << bit):
            slots[bit, mask] = len(slots)

    def grads_copy(kind, s):
        target = (dp + s) % n_dp
        if kind == 0:
            src, dst = g_up_ref.at[target], up_out.at[:, span(dp, units)]
        else:
            src, dst = g_down_ref.at[target], down_out.at[span(dp, units), :]
        return remote(src, dst, grads_sems, (kind, s), {"dp": target})

    def grads_arrival(kind, s):
        source = (dp + n_dp - s) % n_dp
        here = up_out.at[:, span(source, units)] if kind == 0 else down_out.at[span(source, units), :]
        return remote(here, here, grads_sems, (kind, s), {"dp": (dp + s) % n_dp})

    def current(a, bit, mask, b):
        if bit == 0:
            return partials.at[a, mask, b]
        return fold.at[a, slots[bit - 1, mask], b]

    def fold_copy(a, bit, mask, b):
        slot = slots[bit, mask ^ 1 << bit]
        return remote(
            current(a, bit, mask, b), fold.at[a, slot, b], fold_sems, (a, slot, b),
            {"tensor": flipped(tensor, 1 << bit, bits)},
        )

    def fold_arrival(a, bit, mask, b):
        slot = slots[bit, mask]
        here = fold.at[a, slot, b]
        return remote(
            here, here, fold_sems, (a, slot, b), {"tensor": flipped(tensor, 1 << bit, bits)}
        )

    def add_into(ref, other):
        @pl.loop(0, rows // 16)
        def _(i):
            cut = pl.ds(pl.multiple_of(i * 16, 16), 16)
            ref[cut, :] = (
                ref[cut, :].astype(jnp.float32) + other[cut, :].astype(jnp.float32)
            ).astype(ref.dtype)

    def sent_masks(bit):
        masks = [m for m in range(n_tensor) if m % (1 << bit) == 0 and m >> bit & 1]
        return sorted(masks, reverse=True)

    def kept_masks(bit):
        return sorted(range(0, n_tensor, 2 << bit), reverse=True)

    @pl.loop(1, n_dp)
    def _(s):
        weight_block(0, (dp + s) % n_dp)
        grads_copy(0, s).start()

    way = 2 * ((2 * dp) // n_dp) - 1

    def multiply(mask, b):
        cut = span(flipped(tensor, mask, bits) * n_dp + b, rows)
        partials[0, mask, b] = jnp.dot(
            hidden_ref[cut, :], down_ref[...], preferred_element_type=jnp.float32
        ).astype(partials.dtype)
        partials[1, mask, b] = lax.dot_general(
            pre_ref[cut, :], up_ref[...], (((1,), (1,)), ((), ())),
            preferred_element_type=jnp.float32,
        ).astype(partials.dtype)

    def folded(bit, mask, b):
        for a in range(2):
            fold_arrival(a, bit, mask, b).wait_recv()
            add_into(fold.at[a, slots[bit, mask], b], current(a, bit, mask, b))
            if bit + 1 < bits and mask in sent_masks(bit + 1):
                fold_copy(a, bit + 1, mask, b).start()

    for mask in sent_masks(0):
        @pl.loop(0, n_dp)
        def _(i, mask=mask):
            b = (dp + way * (1 + i) + n_dp) % n_dp
            multiply(mask, b)
            for a in range(2):
                fold_copy(a, 0, mask, b).start()

        @pl.loop(0, n_dp)
        def _(i, mask=mask):
            b = (dp + way * (1 + i) + n_dp) % n_dp
            multiply(mask - 1, b)
            folded(0, mask - 1, b)

    for bit in range(1, bits - 1):
        for mask in kept_masks(bit):
            for i in range(n_dp):
                folded(bit, mask, (dp + way * (1 + i) + n_dp) % n_dp)

    def finish(b):
        if bits > 1:
            folded(bits - 1, 0, b)

    last = slots[bits - 1, 0]
    moving = (right, left)

    def line_conditions(side, s):
        return dp + s <= n_dp - 1 if side == 0 else dp >= s

    def behind(side):
        return dp >= 1 if side == 0 else dp <= n_dp - 2

    def line_peer(side):
        return {"dp": (dp + 1) % n_dp if side == 0 else (dp + n_dp - 1) % n_dp}

    def line_copy(a, side, s, relayed):
        target = dp + s if side == 0 else dp - s
        src = moving[side].at[a, s] if relayed else fold.at[a, last, target]
        return remote(src, moving[side].at[a, s - 1], line_sems, (a, side, s - 1), line_peer(side))

    def line_arrival(a, side, s):
        here = moving[side].at[a, s]
        return remote(here, here, line_sems, (a, side, s), line_peer(side))

    for s in range(n_dp - 1, 0, -1):
        weight_block(1, (dp + s) % n_dp)
        for side in range(2):
            @pl.when(jnp.logical_and(line_conditions(side, s), jnp.logical_not(behind(side))))
            def _(side=side, s=s):
                finish(dp + s if side == 0 else dp - s)
                for a in range(2):
                    line_copy(a, side, s, False).start()

            if s <= n_dp - 2:
                @pl.when(jnp.logical_and(line_conditions(side, s), behind(side)))
                def _(side=side, s=s):
                    target = dp + s if side == 0 else dp - s
                    finish(target)
                    for a in range(2):
                        line_arrival(a, side, s).wait_recv()
                        add_into(moving[side].at[a, s], fold.at[a, last, target])
                        line_copy(a, side, s, True).start()
        grads_copy(1, s).start()
    weight_block(0, dp)
    weight_block(1, dp)
    local = [
        pltpu.make_async_copy(g_up_ref.at[dp], up_out.at[:, span(dp, units)], local_sem.at[0]),
        pltpu.make_async_copy(g_down_ref.at[dp], down_out.at[span(dp, units), :], local_sem.at[1]),
    ]
    for copy in local:
        copy.start()
    finish(dp)

    for a in range(2):
        for side in range(2):
            @pl.when(behind(side))
            def _(a=a, side=side):
                line_arrival(a, side, 0).wait_recv()

            @pl.when(jnp.logical_not(behind(side)))
            def _(a=a, side=side):
                moving[side][a, 0] = jnp.zeros((rows, width), moving[side].dtype)

    stat_line[dp] = jnp.zeros(stat_line.shape[1:], jnp.float32)

    @pl.loop(0, rows // 16)
    def _(i):
        cut = pl.ds(pl.multiple_of(i * 16, 16), 16)

        def total(a):
            return (
                fold[a, last, dp, cut, :].astype(jnp.float32)
                + right[a, 0, cut, :].astype(jnp.float32)
                + left[a, 0, cut, :].astype(jnp.float32)
            )

        second_in_ref[cut, :] = (second_ref[cut, :].astype(jnp.float32) - total(0)).astype(
            second_in_ref.dtype
        )
        standard, inv_std = standardize(first_ref[cut, :])
        grad_normed = total(1)
        stat_line[dp, 0:1, :] += jnp.sum(grad_normed * standard, axis=0, keepdims=True)
        stat_line[dp, 1:2, :] += jnp.sum(grad_normed, axis=0, keepdims=True)
        grad_std = grad_normed * gain_ref[...]
        grad_rows = inv_std * (
            grad_std
            - jnp.mean(grad_std, axis=-1, keepdims=True)
            - standard * jnp.mean(grad_std * standard, axis=-1, keepdims=True)
        )
        grad_first_ref[cut, :] = grad_ref[cut, :].astype(jnp.float32) + grad_rows

    def stat_copy(s):
        here = stat_line.at[dp]
        return remote(here, here, stat_sems, s, {"dp": (dp + s) % n_dp})

    def stat_arrival(s):
        here = stat_line.at[(dp + n_dp - s) % n_dp]
        return remote(here, here, stat_sems, s, {"dp": (dp + s) % n_dp})

    for s in range(1, n_dp):
        stat_copy(s).start()
    for s in range(1, n_dp):
        stat_arrival(s).wait_recv()
    sums = stat_line[0]
    for source in range(1, n_dp):
        sums = sums + stat_line[source]
    for bit in range(bits):
        stat_fold[bit, 0] = sums
        copy = remote(
            stat_fold.at[bit, 0], stat_fold.at[bit, 1], pair_sems, bit,
            {"tensor": flipped(tensor, 1 << bit, bits)},
        )
        copy.start()
        copy.wait()
        sums = stat_fold[bit, 0] + stat_fold[bit, 1]
    grad_norm_ref[...] = sums[0:2] * grad_scale

    for s in range(1, n_dp):
        stat_copy(s).wait_send()
        for kind in range(2):
            grads_arrival(kind, s).wait_recv()
            grads_copy(kind, s).wait_send()
    for copy in local:
        copy.wait()
    for bit in range(bits):
        for mask in sent_masks(bit):
            for b in range(n_dp):
                for a in range(2):
                    fold_copy(a, bit, mask, b).wait_send()
    for s in range(n_dp - 1, 0, -1):
        for a in range(2):
            for side in range(2):
                @pl.when(line_conditions(side, s))
                def _(a=a, side=side, s=s):
                    line_copy(a, side, s, s <= n_dp - 2).wait_send()


def standardize(row_data):
    values = row_data.astype(jnp.float32)
    centred = values - jnp.mean(values, axis=-1, keepdims=True)
    inv_std = lax.rsqrt(jnp.mean(centred * centred, axis=-1, keepdims=True) + epsilon)
    return centred * inv_std, inv_std


def fused_kernel(
    n_groups, n_tensor, n_dp, grad_scale,
    first_ref, second_ref, grad_first_in_ref, grad_ref, w_up_ref, w_down_ref, gain_ref, bias_ref,
    second_in_ref, grad_first_ref, grad_norm_ref, up_out, down_out,
    normed_all, grad_all, up_ref, down_ref, hidden_ref, pre_ref, g_up_ref, g_down_ref,
    *scratch,
):
    tensor = lax.axis_index("tensor")
    bits = n_tensor.bit_length() - 1
    column = first_ref.shape[0] * n_dp
    chunk = column // 2
    depth = g_up_ref.shape[1]
    gather_count = 10

    def use(mask):
        base = flipped(tensor, mask, bits)

        @pl.loop(0, column // chunk)
        def _(i):
            cut = span(base * (column // chunk) + i, chunk)
            preact = jnp.dot(
                normed_all[cut, :], up_ref[...], preferred_element_type=jnp.float32
            )
            grad_hidden = lax.dot_general(
                grad_all[cut, :], down_ref[...], (((1,), (1,)), ((), ())),
                preferred_element_type=jnp.float32,
            )
            root = (2.0 / np.pi) ** 0.5
            square = preact * preact
            bend = jnp.tanh(root * (preact + 0.044715 * (square * preact)))
            gate = 0.5 * (1.0 + bend)
            hidden_ref[cut, :] = (preact * gate).astype(hidden_ref.dtype)
            slope = gate + (0.5 * preact) * (1.0 - bend * bend) * (
                root * (1.0 + 3.0 * 0.044715 * square)
            )
            pre_ref[cut, :] = (grad_hidden * slope).astype(pre_ref.dtype)

    def weight_block(kind, target):
        cut = span(target, depth)
        if kind == 0:
            g_up_ref[target] = contract_tokens(normed_all[:, cut], pre_ref[...]).astype(g_up_ref.dtype)
        else:
            g_down_ref[target] = contract_tokens(hidden_ref[...], grad_all[:, cut]).astype(
                g_down_ref.dtype
            )

    gather_tokens(
        n_groups, n_tensor, n_dp, use,
        first_ref, grad_ref, w_up_ref, w_down_ref, gain_ref, bias_ref,
        normed_all, grad_all, up_ref, down_ref, *scratch[:gather_count],
    )
    scatter_sums(
        n_groups, n_tensor, n_dp, grad_scale, weight_block,
        hidden_ref, pre_ref, up_ref, down_ref, g_up_ref, g_down_ref,
        first_ref, second_ref, grad_first_in_ref, gain_ref,
        second_in_ref, grad_first_ref, grad_norm_ref, up_out, down_out, *scratch[gather_count:],
    )


ANY = pl.BlockSpec(memory_space=pl.ANY)
VMEM = pl.BlockSpec(memory_space=pltpu.VMEM)
DMA = pltpu.SemaphoreType.DMA


def spread_body(sizes, first_out, second_out, grad_first, grad_second, w_up, w_down, norm_gain, norm_bias):
    n_groups, n_tensor, n_dp = sizes
    rows, width = first_out.shape
    tokens = rows * n_tensor * n_dp
    units = w_up.shape[1] // n_dp
    bits = n_tensor.bit_length() - 1
    half = jnp.bfloat16
    grad_scale = tokens ** (-0.5)
    gain, bias = norm_gain.reshape(1, -1), norm_bias.reshape(1, -1)
    depth = w_up.shape[0]
    second_in, grad_first_in, grad_norm, up_out, down_out = pl.pallas_call(
        functools.partial(fused_kernel, n_groups, n_tensor, n_dp, grad_scale),
        out_shape=(
            jax.ShapeDtypeStruct((rows, width), half),
            jax.ShapeDtypeStruct((rows, width), jnp.float32),
            jax.ShapeDtypeStruct((2, width), jnp.float32),
            jax.ShapeDtypeStruct(w_up.shape, half),
            jax.ShapeDtypeStruct(w_down.shape, half),
        ),
        in_specs=[VMEM] * 8,
        out_specs=(VMEM,) * 3 + (ANY,) * 2,
        scratch_shapes=[
            pltpu.VMEM((tokens, width), half),
            pltpu.VMEM((tokens, width), half),
            pltpu.VMEM((width, units), half),
            pltpu.VMEM((units, width), half),
            pltpu.VMEM((tokens, units), half),
            pltpu.VMEM((tokens, units), half),
            pltpu.VMEM((n_dp, depth, units), half),
            pltpu.VMEM((n_dp, units, depth), half),
        ]
        + [pltpu.VMEM((rows, width), half), DMA((4,))]
        + [DMA((2, 2, n_dp))] * 2
        + [DMA((2, n_tensor, 2 * n_dp - 1))] * 2
        + [DMA((2, n_dp))] * 2
        + [DMA((2, n_dp, n_groups))] * 2
        + [
            pltpu.VMEM((2, n_tensor, n_dp, rows, width), half),
            pltpu.VMEM((2, n_tensor - 1, n_dp, rows, width), half),
            pltpu.VMEM((2, n_dp - 1, rows, width), half),
            pltpu.VMEM((2, n_dp - 1, rows, width), half),
            pltpu.VMEM((n_dp, 8, width), jnp.float32),
            pltpu.VMEM((bits, 2, 8, width), jnp.float32),
            DMA((2,)),
        ]
        + [DMA((2, n_tensor - 1, n_dp))] * 2
        + [DMA((2, 2, n_dp - 1))] * 2
        + [DMA((2, n_dp))] * 2
        + [DMA((n_dp,))] * 2
        + [DMA((bits,))] * 2,
        compiler_params=pltpu.CompilerParams(
            collective_id=0, has_side_effects=True, vmem_limit_bytes=60 << 20
        ),
        name="spread_backward",
    )(first_out, second_out, grad_first, grad_second, w_up, w_down, gain, bias)
    grad_up = up_out.astype(jnp.float32) * grad_scale
    grad_down = down_out.astype(jnp.float32) * grad_scale
    return second_in, grad_first_in, grad_up, grad_down, grad_norm


def choose(sizes, *args):
    first_out, w_up = args[0], args[4]
    n_groups, n_tensor, n_dp = sizes
    tokens = first_out.shape[0] * n_tensor * n_dp
    fits = (
        n_tensor > 1
        and n_dp > 1
        and n_dp % 2 == 0
        and n_tensor & (n_tensor - 1) == 0
        and w_up.shape[1] % (n_dp * n_groups * 128) == 0
        and w_up.shape[0] % (n_groups * 128) == 0
    )
    if fits and tokens <= w_up.shape[1]:
        return spread_body(sizes, *args)
    return body(*args)


def solution(mesh):
    in_specs = (
        P(("groups", "tensor", "dp"), None),
        P(("groups", "tensor", "dp"), None),
        P(("groups", "tensor", "dp"), None),
        P(("groups", "tensor", "dp"), None),
        P("dp", "tensor"),
        P("tensor", "dp"),
        P(),
        P(),
    )
    out_specs = (
        P(("groups", "tensor", "dp"), None),
        P(("groups", "tensor", "dp"), None),
        P(("groups", "dp"), "tensor"),
        P(("groups", "tensor"), "dp"),
        P("groups", None),
    )
    sizes = tuple(mesh.shape[name] for name in ("groups", "tensor", "dp"))
    return jax.shard_map(functools.partial(choose, sizes), mesh=mesh, in_specs=in_specs, out_specs=out_specs, check_vma=False)
```
